32 devices in a mesh: grp: 2 (over y), rot: 4 (over z), shell: 2 (over x), ang: 2 (over core).
Axes of the slice: x: 2, y: 2, z: 4, core: 2. Of those that a mesh axis runs over, the one named last changes fastest.
Arguments:
- images: float32 [2, 128, 64, 2048], P(None, 'shell', 'ang', ('grp', 'rot')), parts along dimension 3, may hold values from -16 to 16
- references: bfloat16 [2, 128, 64, 2048], P(None, 'shell', 'ang', ('grp', 'rot')), parts along dimension 3, may hold values from -4 to 4
- noise_weight: float32 [256], P(('grp', 'shell')), parts along dimension 0, may hold values from 0.004 to 0.03
- euler_angles: float32 [3, 2048], P(None, ('grp', 'rot')), parts along dimension 1, may hold values from -3.140625 to 3.140625
- candidate_count: int32 [16, 4], P(('grp', 'rot')), parts along dimension 0, may hold values from 0 to 8, as said below
- candidate_rotation: int32 [16, 4, 8], P(('grp', 'rot')), parts along dimension 0, may hold values from 0 to 255, as said below
- image_order: int32 [2048], P(('grp', 'rot')), parts along dimension 0, may hold values from 0 to 255, as said below
Outputs:
- coefficients: float32 [2048, 2, 128], P(('grp', 'rot', 'ang'), None, 'shell'), parts along dimension 0
- log_evidence: float32 [2048], P(('grp', 'rot')), parts along dimension 0
The draws below stay inside these ranges and needn't reach their ends.
There are 2 independent parts, one for each index of `grp`. The reference program is written for one: setup_inputs(seed, part) draws one part's arguments, and reference() takes and returns one part's arrays. A program takes and returns all parts, laid end to end along the dimension named above; each array names one. Nothing has to cross between parts.
Inputs may be any that keep to these rules, and one draw needn't show every extreme that they name: `image_order`: within each device's 256 entries, a permutation of 0 to 255. `candidate_count`: for the 2 blocks of one device and one owner the counts add up to at most 8; in every draw one owner, drawn from the seed, gets exactly 8 from every device, with 8 in one block of each device; every block has two or more candidates in all. `candidate_rotation`: the 8 entries of one block and owner are distinct; entries at or past the count are not used.
All inputs are finite; a program needn't handle non-finite values.
Results may differ from the reference program's by a relative error of at most 0.0074.
Values may be sent and summed in bfloat16 or wider, within the bound.
No kernel may reach another device: no remote copies, remote signals or barrier semaphores. Data moves between devices by JAX's collectives and lax.ppermute only.
A program may use at most 64 MiB of HBM per device.

```python
import math
import jax
import jax.numpy as jnp
from jax import lax

SHELLS = 128
ANGLES = 64
ORDER = 32
BLOCK = 128
CPO = 8
IMG_DEV = 256
ROT_DEV = 256
COEF = 1024
BLK_DEV = 2
OWNERS = 4
IMAGES = 1024
BLOCKS = 8
ROTS = 1024


def permute_one(shuffle_key):
    return jax.random.permutation(shuffle_key, IMG_DEV)


def shared_draw(key):
    subkeys = jax.random.split(jax.random.fold_in(key, 4099), 9)
    references = jnp.clip(jax.random.normal(subkeys[0], (2, SHELLS, ANGLES, ROTS), jnp.float32), -4.0, 4.0)
    noise_weight = jnp.exp(jax.random.uniform(subkeys[2], (SHELLS,), jnp.float32, math.log(0.004), math.log(0.03)))
    popular = jax.random.randint(subkeys[3], (OWNERS,), 0, 4)
    raw_draw = jax.random.randint(subkeys[4], (OWNERS, BLK_DEV, OWNERS), 0, CPO // 2)
    counts = jnp.minimum(CPO // 2, 1 + raw_draw * popular[None, None, :] // 2)
    forced_owner = jax.random.randint(subkeys[5], (), 0, OWNERS)
    forced_block = jax.random.randint(subkeys[6], (OWNERS,), 0, BLK_DEV)
    block_rank = (jnp.arange(BLK_DEV)[None, :] - forced_block[:, None]) % BLK_DEV
    forced_counts = jnp.where(block_rank == 0, CPO, jnp.where(block_rank <= BLK_DEV - 2, CPO // 2, 0))
    forced_mask = (jnp.arange(OWNERS) == forced_owner)[None, None, :]
    counts = jnp.where(forced_mask, forced_counts[:, :, None], counts).reshape(BLOCKS, OWNERS).astype(jnp.int32)
    scores = jax.random.randint(subkeys[7], (BLOCKS, OWNERS, ROT_DEV), 0, 1 << 20) * ROT_DEV + jnp.arange(ROT_DEV)
    indices = lax.top_k(scores.astype(jnp.int32), CPO)[1].astype(jnp.int32)
    shuffle_keys = jax.random.split(subkeys[8], OWNERS)
    ordering = jax.vmap(permute_one)(shuffle_keys).reshape(IMAGES).astype(jnp.int32)
    return (references, noise_weight, counts, indices, ordering)


def draw_references(key, part):
    return shared_draw(key)[0].astype(jnp.bfloat16)


def draw_noise_weight(key, part):
    return shared_draw(key)[1]


def draw_candidate_count(key, part):
    return shared_draw(key)[2]


def draw_candidate_rotation(key, part):
    return shared_draw(key)[3]


def draw_image_order(key, part):
    return shared_draw(key)[4]


def draw_images(key, part):
    subkeys = jax.random.split(jax.random.fold_in(key, 7919), 3)
    return jnp.clip(jax.random.normal(subkeys[2], (2, SHELLS, ANGLES, IMAGES), jnp.float32), -6.0, 6.0)


def setup_inputs(seed: int = 0, part: int = 0) -> dict:
    arg_keys = jax.random.split(jax.random.key(seed), 8)
    own_keys = jax.random.split(jax.random.fold_in(arg_keys[7], part), 8)
    images = draw_images(jax.random.fold_in(jax.random.fold_in(arg_keys[7], part), 71), part)
    references = draw_references(jax.random.fold_in(jax.random.fold_in(arg_keys[7], part), 71), part)
    noise_weight = draw_noise_weight(jax.random.fold_in(jax.random.fold_in(arg_keys[7], part), 71), part)
    euler_angles = jnp.clip(jax.random.uniform(own_keys[3], (3, ROTS), jnp.float32, -3.140625, 3.140625), -3.140625, 3.140625)
    candidate_count = draw_candidate_count(jax.random.fold_in(jax.random.fold_in(arg_keys[7], part), 71), part)
    candidate_rotation = draw_candidate_rotation(jax.random.fold_in(jax.random.fold_in(arg_keys[7], part), 71), part)
    image_order = draw_image_order(jax.random.fold_in(jax.random.fold_in(arg_keys[7], part), 71), part)
    return {"images": images, "references": references, "noise_weight": noise_weight, "euler_angles": euler_angles, "candidate_count": candidate_count, "candidate_rotation": candidate_rotation, "image_order": image_order}


def legendre_constants(degrees):
    first_coef = []
    second_coef = []
    for degree in range(degrees):
        first_line = []
        second_line = []
        for azimuth in range(degrees):
            if azimuth < degree:
                first_line.append(math.sqrt((4.0 * degree * degree - 1.0) / (degree * degree - azimuth * azimuth)))
                lower_term = max((degree - 1.0) ** 2 - azimuth * azimuth, 0.0)
                lower_den = max(4.0 * (degree - 1.0) ** 2 - 1.0, 1.0)
                second_line.append(math.sqrt(lower_term / lower_den))
            else:
                first_line.append(0.0)
                second_line.append(0.0)
        first_coef.append(first_line)
        second_coef.append(second_line)
    diagonal = []
    running = 1.0
    for degree in range(degrees):
        if degree > 0:
            running = running * (2.0 * degree - 1.0) / (2.0 * degree)
        diagonal.append(math.sqrt((2.0 * degree + 1.0) / (4.0 * math.pi) * running))
    pick_rows = []
    pick_trig = []
    factors = []
    for degree in range(degrees):
        pick_rows.append(degree * degrees)
        pick_trig.append(0)
        factors.append(1.0)
        for azimuth in range(1, degree + 1):
            for parity in range(2):
                pick_rows.append(degree * degrees + azimuth)
                pick_trig.append(parity * degrees + azimuth)
                factors.append(math.sqrt(2.0))
    return (first_coef, second_coef, diagonal, pick_rows, pick_trig, factors)

def harmonic_table(euler_angles, angle_ids, angle_count, degrees):
    first_coef, second_coef, diagonal, pick_rows, pick_trig, factors = legendre_constants(degrees)
    in_plane = 2.0 * math.pi / angle_count * angle_ids.astype(jnp.float32)
    phases = in_plane[:, None] + euler_angles[2][None, :]
    cos_phase = jnp.cos(phases)
    sin_phase = jnp.sin(phases)
    cos_alpha = jnp.cos(euler_angles[0])[None, :]
    sin_alpha = jnp.sin(euler_angles[0])[None, :]
    cos_beta = jnp.cos(euler_angles[1])[None, :]
    sin_beta = jnp.sin(euler_angles[1])[None, :]
    along_x = (cos_alpha * cos_beta * cos_phase - sin_alpha * sin_phase).reshape(-1)
    along_y = (sin_alpha * cos_beta * cos_phase + cos_alpha * sin_phase).reshape(-1)
    along_z = (-sin_beta * cos_phase).reshape(-1)

    def trig_step(carry, unused):
        real_part, imag_part = carry
        return ((along_x * real_part - along_y * imag_part, along_x * imag_part + along_y * real_part), carry)
    unused_carry, (real_rows, imag_rows) = lax.scan(trig_step, (jnp.ones_like(along_x), jnp.zeros_like(along_x)), None, length=degrees)
    azimuths = jnp.arange(degrees)
    diag_col = jnp.asarray(diagonal, jnp.float32)[:, None]

    def legendre_step(carry, inputs):
        previous, earlier = carry
        degree, coef_first, coef_second = inputs
        current = coef_first[:, None] * (along_z[None, :] * previous - coef_second[:, None] * earlier)
        current = jnp.where((azimuths == degree)[:, None], diag_col, current)
        return ((current, previous), current)
    zero_rows = jnp.zeros((degrees, along_z.shape[0]), jnp.float32)
    unused_state, stacked = lax.scan(legendre_step, (zero_rows, zero_rows), (jnp.arange(degrees), jnp.asarray(first_coef, jnp.float32), jnp.asarray(second_coef, jnp.float32)))
    legendre = stacked.reshape(degrees * degrees, -1)
    trig_rows = jnp.concatenate([real_rows, imag_rows], axis=0)
    table_rows = jnp.take(legendre, jnp.asarray(pick_rows, jnp.int32), axis=0) * jnp.take(trig_rows, jnp.asarray(pick_trig, jnp.int32), axis=0) * jnp.asarray(factors, jnp.float32)[:, None]
    return table_rows.astype(jnp.bfloat16)

def reference(images, references, noise_weight, euler_angles, candidate_count, candidate_rotation, image_order):
    features = 2 * SHELLS * ANGLES
    shell_scale = jnp.broadcast_to(noise_weight[None, :, None], (2, SHELLS, ANGLES)).reshape(features)
    weighted = (images.reshape(features, IMAGES) * shell_scale[:, None]).astype(jnp.bfloat16)
    slice_table = references.reshape(features, ROTS)
    slot_ids = jnp.arange(CPO)
    owner_ids = jnp.arange(OWNERS)

    def one_block(running_sum, block_id):
        first_pos = block_id * BLOCK
        device = first_pos // IMG_DEV
        members = device * IMG_DEV + lax.dynamic_slice_in_dim(image_order, first_pos, BLOCK)
        columns = jnp.take(weighted, members, axis=1).astype(jnp.float32)
        rotation_ids = (owner_ids[:, None] * ROT_DEV + candidate_rotation[block_id]).reshape(-1)
        is_valid = (slot_ids[None, :] < candidate_count[block_id][:, None]).reshape(-1)
        slices = jnp.take(slice_table, rotation_ids, axis=1).astype(jnp.float32)
        slot_norms = lax.optimization_barrier(jnp.sum(jnp.square(slices) * shell_scale[:, None], axis=0))
        scores = 2.0 * lax.dot_general(columns, slices, (((0,), (0,)), ((), ())), precision=lax.Precision.HIGHEST, preferred_element_type=jnp.float32) - slot_norms[None, :]
        masked = jnp.where(is_valid[None, :], scores, -jnp.inf)
        highest = lax.optimization_barrier(jnp.max(masked, axis=1))
        totals = lax.optimization_barrier(jnp.sum(jnp.exp(masked - highest[:, None]), axis=1))
        evidence = highest + jnp.log(totals)
        weights = jnp.exp(masked - evidence[:, None]).astype(jnp.bfloat16).astype(jnp.float32)
        averages = jnp.dot(columns, weights, precision=lax.Precision.HIGHEST, preferred_element_type=jnp.float32).astype(jnp.bfloat16)
        running_sum = running_sum.at[:, rotation_ids].add(averages.astype(jnp.float32))
        return (running_sum, evidence)
    running_sum, evidence = lax.scan(one_block, jnp.zeros((features, ROTS), jnp.float32), jnp.arange(BLOCKS).astype(jnp.int32))
    positions = jnp.arange(IMAGES)
    image_ids = positions // IMG_DEV * IMG_DEV + image_order
    log_evidence = jnp.zeros((IMAGES,), jnp.float32).at[image_ids].set(evidence.reshape(-1))
    rotation_average = running_sum.astype(jnp.bfloat16).reshape(2 * SHELLS, ANGLES, ROTS)

    def one_angle(coef_sum, angle_id):
        harmonics = harmonic_table(euler_angles, angle_id[None], ANGLES, ORDER).astype(jnp.float32)
        angle_plane = lax.dynamic_index_in_dim(rotation_average, angle_id, 1, keepdims=False).astype(jnp.float32)
        return (coef_sum + lax.dot_general(harmonics, angle_plane, (((1,), (1,)), ((), ())), precision=lax.Precision.HIGHEST, preferred_element_type=jnp.float32), None)
    coefficients, unused = lax.scan(one_angle, jnp.zeros((COEF, 2 * SHELLS), jnp.float32), jnp.arange(ANGLES).astype(jnp.int32))
    return (coefficients.reshape(COEF, 2, SHELLS), log_evidence)
```

```python
import functools
import math

import jax
import jax.numpy as jnp
from jax import lax
from jax.experimental import pallas as pl
from jax.experimental.pallas import tpu as pltpu
from jax.sharding import PartitionSpec as P

ORDER = 32
COEF = ORDER * ORDER
LANES = 128
SUBLANES = 8
TILE = SUBLANES * LANES
MIB = 1 << 20


SMEM = pl.BlockSpec(memory_space=pltpu.SMEM)
VMEM = pl.BlockSpec(memory_space=pltpu.VMEM)
F32 = jnp.float32
BF16 = jnp.bfloat16
I32 = jnp.int32


def struct(shape, dtype):
    return jax.ShapeDtypeStruct(shape, dtype)


def iota(shape, dim):
    return lax.broadcasted_iota(I32, shape, dim)


def slot_block(count_ref, blocks, owner, position):
    found = jnp.full_like(position, -1)
    start = 0
    for block in range(blocks):
        stop = start + count_ref[block, owner]
        found = jnp.where((position >= start) & (position < stop), block, found)
        start = stop
    return found


def compact_body(rotation_ref, count_ref, out_ref):
    blocks, owners, slots = rotation_ref.shape

    def one_owner(owner, carry):
        for position in range(slots):
            value = jnp.int32(-1)
            start = jnp.int32(0)
            for block in range(blocks):
                count = count_ref[block, owner]
                local = position - start
                inside = (local >= 0) & (local < count)
                entry = rotation_ref[block, owner, jnp.clip(local, 0, slots - 1)]
                value = jnp.where(inside, entry, value)
                start = start + count
            out_ref[owner, position] = value
        return carry

    lax.fori_loop(0, owners, one_owner, 0)


def select_body(low_ref, high_ref, reference_ref, euler_ref, *out_refs):
    owners = len(out_refs)
    half = low_ref.shape[0]
    slots = low_ref.shape[2]
    features, rotations = reference_ref.shape
    me = lax.axis_index("rot")
    row = iota((slots, LANES), 0)
    groups = []
    for turn in range(owners):
        asked = low_ref if turn < half else high_ref
        group = jnp.full((slots, LANES), -1, I32)
        for position in range(slots):
            group = jnp.where(row == position, asked[turn % half, me, position], group)
        groups.append(group)
    wanted = jnp.concatenate(groups, axis=0)
    wanted = jnp.concatenate([wanted] * (rotations // LANES), axis=1)
    chosen = jnp.where(wanted == iota(wanted.shape, 1), 1.0, 0.0).astype(BF16)
    picked = lax.dot_general(
        chosen, reference_ref[...], (((1,), (1,)), ((), ())), preferred_element_type=F32
    )
    line = iota((SUBLANES, rotations), 0)
    rest = jnp.where(
        line == 0,
        euler_ref[0:1, :],
        jnp.where(line == 1, euler_ref[1:2, :], jnp.where(line == 2, euler_ref[2:3, :], 0.0)),
    )
    terms = []
    for unused in range(3):
        term = rest.astype(BF16).astype(F32)
        terms.append(term)
        rest = rest - term
    terms.append(jnp.zeros((LANES - 3 * SUBLANES, rotations), F32))
    angles = lax.dot_general(
        chosen,
        jnp.concatenate(terms, axis=0).astype(BF16),
        (((1,), (1,)), ((), ())),
        preferred_element_type=F32,
    )
    for turn, out_ref in enumerate(out_refs):
        rows = slice(turn * slots, (turn + 1) * slots)
        out_ref[:, :features] = picked[rows].astype(BF16)
        out_ref[:, features:] = angles[rows].astype(BF16)


def weigh_body(angles_here, block_size, noise_ref, order_ref, *refs):
    image_refs = refs[:-3]
    natural_ref, turned_ref, block_ref = refs[-3:]
    images = natural_ref.shape[1]
    lines = natural_ref.shape[0] // angles_here
    shells = noise_ref.shape[0]
    step = pl.program_id(0)
    row = iota((lines, LANES), 0)
    column = jnp.zeros((lines, LANES), F32)
    for line in range(lines):
        weight = noise_ref[lax.rem(step * lines + line, shells)]
        column = jnp.where(row == line, weight, column)
        rows = slice(line * angles_here, (line + 1) * angles_here)
        for side, image_ref in enumerate(image_refs):
            lanes = slice(side * LANES, (side + 1) * LANES)
            natural_ref[rows, lanes] = (image_ref[rows, :] * weight).astype(BF16)
    for angle in range(angles_here):
        for side, image_ref in enumerate(image_refs):
            lanes = slice(side * LANES, (side + 1) * LANES)
            plane = image_ref[pl.ds(angle, lines, stride=angles_here), :]
            turned_ref[angle, :, lanes] = (plane * column).astype(BF16)

    @pl.when(step == 0)
    def find_blocks():
        same = jnp.where(order_ref[...] == iota((images, images), 0), 1.0, 0.0).astype(BF16)
        block_of = (iota((SUBLANES, images), 1) // block_size).astype(F32).astype(BF16)
        block_ref[...] = lax.dot_general(
            block_of, same, (((1,), (1,)), ((), ())), preferred_element_type=F32
        )


def score_body(noise_ref, natural_ref, *refs):
    slice_refs = refs[:-2]
    score_ref, euler_ref = refs[-2:]
    features = natural_ref.shape[0]
    slices = jnp.concatenate([ref[:, :features].astype(F32) for ref in slice_refs], axis=0)
    norms = jnp.sum(slices * slices * noise_ref[...], axis=1, keepdims=True)
    products = jnp.dot(slices.astype(BF16), natural_ref[...], preferred_element_type=F32)
    score_ref[...] = 2.0 * products - norms
    terms = jnp.concatenate([ref[:, features:].astype(F32) for ref in slice_refs], axis=0)
    slots = terms.shape[0]
    terms = terms.astype(BF16)
    repeats = max(1, slots // LANES)
    line = iota((SUBLANES, LANES), 0)
    planes = [jnp.zeros((SUBLANES, LANES), F32)] * 3
    for repeat in range(repeats):
        place = lax.rem(repeat * LANES + iota((slots, LANES), 1), slots)
        spread = jnp.where(place == iota((slots, LANES), 0), 1.0, 0.0).astype(BF16)
        rows = lax.dot_general(
            terms, spread, (((0,), (0,)), ((), ())), preferred_element_type=F32
        )
        whole = rows[:8] + rows[8:16] + rows[16:24]
        here = lax.rem(line, repeats) == repeat
        planes = [
            jnp.where(here, whole[axis : axis + 1, :], planes[axis]) for axis in range(3)
        ]
    for axis in range(3):
        euler_ref[axis] = planes[axis]


def harmonic_constants():
    first = {}
    second = {}
    for degree in range(ORDER):
        for azimuth in range(degree):
            first[degree, azimuth] = math.sqrt(
                (4.0 * degree * degree - 1.0) / (degree * degree - azimuth * azimuth)
            )
            lower = max((degree - 1.0) ** 2 - azimuth * azimuth, 0.0)
            second[degree, azimuth] = math.sqrt(lower / max(4.0 * (degree - 1.0) ** 2 - 1.0, 1.0))
    diagonal = []
    running = 1.0
    for degree in range(ORDER):
        if degree > 0:
            running = running * (2.0 * degree - 1.0) / (2.0 * degree)
        diagonal.append(math.sqrt((2.0 * degree + 1.0) / (4.0 * math.pi) * running))
    return first, second, diagonal


def harmonic_body(slots, angles_here, angle_count, euler_ref, out_ref, rows_ref):
    first, second, diagonal = harmonic_constants()
    tile = (SUBLANES, LANES)
    column = pl.program_id(0) * TILE + iota(tile, 0) * LANES + iota(tile, 1)
    angle = lax.axis_index("ang") * angles_here + column // slots
    phase = 2.0 * math.pi / angle_count * angle.astype(F32) + euler_ref[2]
    cos_phase = jnp.cos(phase)
    sin_phase = jnp.sin(phase)
    cos_alpha = jnp.cos(euler_ref[0])
    sin_alpha = jnp.sin(euler_ref[0])
    cos_beta = jnp.cos(euler_ref[1])
    sin_beta = jnp.sin(euler_ref[1])
    along_x = cos_alpha * cos_beta * cos_phase - sin_alpha * sin_phase
    along_y = sin_alpha * cos_beta * cos_phase + cos_alpha * sin_phase
    along_z = -sin_beta * cos_phase

    def put(index, value):
        rows_ref[index * SUBLANES : (index + 1) * SUBLANES, :] = value

    real_part = jnp.ones(tile, F32)
    imag_part = jnp.zeros(tile, F32)
    for azimuth in range(ORDER):
        real_scaled = real_part * math.sqrt(2.0)
        imag_scaled = imag_part * math.sqrt(2.0)
        earlier = None
        current = None
        for degree in range(azimuth, ORDER):
            if degree == azimuth:
                value = jnp.full(tile, diagonal[azimuth], F32)
            elif degree == azimuth + 1:
                value = (first[degree, azimuth] * along_z) * current
            else:
                value = first[degree, azimuth] * (
                    along_z * current - second[degree, azimuth] * earlier
                )
            earlier, current = current, value
            if azimuth == 0:
                put(degree * degree, value)
            else:
                put(degree * degree + 2 * azimuth - 1, value * real_scaled)
                put(degree * degree + 2 * azimuth, value * imag_scaled)
        real_part, imag_part = (
            along_x * real_part - along_y * imag_part,
            along_x * imag_part + along_y * real_part,
        )
    for part in range(SUBLANES):
        out_ref[:, part * LANES : (part + 1) * LANES] = rows_ref[
            pl.ds(part, COEF, stride=SUBLANES), :
        ].astype(BF16)


def finish_body(
    angles_here, count_ref, block_ref, turned_ref, harmonic_ref, *refs
):
    blocks, owners = count_ref.shape
    evidence_ref, mine_ref, theirs_ref, average_ref, coef_ref = refs[-5:]
    sums = [ref[...] for ref in refs[:-5]]
    while len(sums) > 1:
        sums = [sums[i] + sums[i + 1] for i in range(0, len(sums), 2)]
    scores = sums[0]
    total, images = scores.shape
    slots = total // owners
    me = lax.axis_index("rot")
    ang = lax.axis_index("ang")
    position = iota((slots, images), 0)
    groups = []
    for turn in range(owners):
        groups.append(slot_block(count_ref, blocks, lax.bitwise_xor(me, turn), position))
    owner_block = jnp.concatenate(groups, axis=0).astype(F32)
    valid = owner_block == block_ref[0:1, :]
    masked = jnp.where(valid, scores, -jnp.inf)
    highest = jnp.max(masked, axis=0, keepdims=True)
    totals = jnp.sum(jnp.exp(masked - highest), axis=0, keepdims=True)
    evidence = highest + jnp.log(totals)
    evidence_ref[...] = evidence
    weights = jnp.where(valid, jnp.exp(masked - evidence), 0.0).astype(BF16)
    averages = lax.dot_general(
        weights, turned_ref[...], (((1,), (1,)), ((), ())), preferred_element_type=F32
    ).astype(BF16)
    lines = turned_ref.shape[0] // angles_here
    for angle in range(angles_here):
        average_ref[angle * total : (angle + 1) * total, :] = averages[
            :, angle * lines : (angle + 1) * lines
        ]
    coef_ref[...] = jnp.dot(harmonic_ref[...], average_ref[...], preferred_element_type=F32)
    parts = coef_ref.shape[0] // (owners * mine_ref.shape[1])
    span = mine_ref.shape[1]
    for turn in range(owners):
        owner = lax.bitwise_xor(me, turn)
        here = pl.multiple_of((owner * parts + ang) * span, span)
        there = pl.multiple_of((owner * parts + (parts - 1 - ang)) * span, span)
        mine_ref[turn] = coef_ref[pl.ds(here, span), :]
        theirs_ref[turn] = coef_ref[pl.ds(there, span), :]


def pair_body(link, mine_ref, other_ref, *out_refs):
    for turn, out_ref in enumerate(out_refs):
        out_ref[...] = (mine_ref[turn] + other_ref[turn]).astype(out_ref.dtype)


def last_body(*refs):
    out_ref = refs[-1]
    total = refs[0][...]
    for ref in refs[1:-1]:
        total = total + ref[...].astype(F32)
    out_ref[...] = total.T


def block_at(side, step):
    return step, side


def params(limit, **more):
    return pltpu.CompilerParams(vmem_limit_bytes=int(min(limit, 60 * MIB)), **more)


def swap(array, axis, size, turn):
    return lax.ppermute(array, axis, [(i, i ^ turn) for i in range(size)])


def per_device(
    images, references, noise_weight, euler_angles, candidate_count, candidate_rotation, image_order
):
    owners = lax.axis_size("rot")
    angle_parts = lax.axis_size("ang")
    shell_parts = lax.axis_size("shell")
    parts, shells_here, angles_here, images_here = images.shape
    lines = parts * shells_here
    features = lines * angles_here
    rotations_here = references.shape[3]
    blocks_here, unused, slots = candidate_rotation.shape
    total = owners * slots
    wide = features + LANES
    columns = angles_here * total
    span = COEF // (owners * angle_parts)
    link = BF16

    request = pl.pallas_call(
        compact_body,
        out_shape=struct((owners, slots), I32),
        in_specs=[SMEM, SMEM],
        out_specs=SMEM,
        name="compact",
    )(candidate_rotation, candidate_count)
    known = request[None]
    turn = 1
    while turn < owners // 2:
        known = jnp.concatenate([known, swap(known, "rot", owners, turn)], axis=0)
        turn *= 2
    far = swap(known, "rot", owners, turn)

    chosen = pl.pallas_call(
        select_body,
        out_shape=[struct((slots, wide), BF16)] * owners,
        in_specs=[SMEM, SMEM, VMEM, VMEM],
        out_specs=[VMEM] * owners,
        compiler_params=params(features * rotations_here * 2 + total * wide * 8 + 4 * MIB),
        name="select",
    )(known, far, references.reshape(features, rotations_here), euler_angles)
    slices = [chosen[0]] + [swap(chosen[k], "rot", owners, k) for k in range(1, owners)]

    chunk = 16
    sides = images_here // LANES
    natural, turned, image_block = pl.pallas_call(
        functools.partial(weigh_body, angles_here, images_here // blocks_here),
        grid=(lines // chunk,),
        out_shape=[
            struct((features, images_here), BF16),
            struct((angles_here, lines, images_here), BF16),
            struct((SUBLANES, images_here), F32),
        ],
        in_specs=[
            SMEM,
            pl.BlockSpec((1, images_here), lambda i: (0, 0)),
        ]
        + [
            pl.BlockSpec((chunk * angles_here, LANES), functools.partial(block_at, side))
            for side in range(sides)
        ],
        out_specs=[
            pl.BlockSpec((chunk * angles_here, images_here), lambda i: (i, 0)),
            pl.BlockSpec((angles_here, chunk, images_here), lambda i: (0, i, 0)),
            pl.BlockSpec((SUBLANES, images_here), lambda i: (0, 0)),
        ],
        cost_estimate=pl.CostEstimate(
            flops=4 * features * images_here, bytes_accessed=8 * features * images_here, transcendentals=0
        ),
        compiler_params=params(8 * chunk * angles_here * images_here * 4),
        name="weigh",
    )(noise_weight, image_order[None], *[images.reshape(features, images_here)] * sides)

    noise_row = jnp.broadcast_to(
        noise_weight[None, :, None], (parts, shells_here, angles_here)
    ).reshape(1, features)
    partial, eulers = pl.pallas_call(
        score_body,
        out_shape=[struct((total, images_here), F32), struct((3, SUBLANES, LANES), F32)],
        in_specs=[VMEM] * (2 + owners),
        out_specs=[VMEM] * 2,
        compiler_params=params(features * images_here * 2 + total * wide * 12 + 4 * MIB),
        name="score",
    )(noise_row, natural, *slices)

    count = shell_parts * angle_parts
    shares = [partial] + [
        lax.ppermute(partial, ("shell", "ang"), [(i, i ^ k) for i in range(count)])
        for k in range(1, count)
    ]

    harmonics = pl.pallas_call(
        functools.partial(harmonic_body, total, angles_here, angles_here * angle_parts),
        grid=(columns // TILE,),
        out_shape=struct((COEF, columns), BF16),
        in_specs=[pl.BlockSpec((3, SUBLANES, LANES), lambda i: (0, 0, 0))],
        out_specs=pl.BlockSpec((COEF, TILE), lambda i: (0, i)),
        scratch_shapes=[pltpu.VMEM((COEF * SUBLANES, LANES), F32)],
        cost_estimate=pl.CostEstimate(
            flops=8 * COEF * columns, bytes_accessed=2 * COEF * columns, transcendentals=6 * columns
        ),
        compiler_params=params(12 * MIB),
        name="harmonics",
    )(eulers)

    evidence, mine, theirs = pl.pallas_call(
        functools.partial(finish_body, angles_here),
        out_shape=[
            struct((1, images_here), F32),
            struct((owners, span, lines), F32),
            struct((owners, span, lines), F32),
        ],
        in_specs=[SMEM] + [VMEM] * (3 + count),
        out_specs=[VMEM] * 3,
        scratch_shapes=[pltpu.VMEM((columns, lines), BF16), pltpu.VMEM((COEF, lines), F32)],
        compiler_params=params(
            features * images_here * 2 + COEF * columns * 2 + total * features * 8
            + columns * lines * 4 + COEF * lines * 16 + 4 * MIB
        ),
        name="finish",
    )(candidate_count, image_block, turned.reshape(features, images_here), harmonics, *shares)

    other = swap(theirs, "ang", angle_parts, 1)
    sums = pl.pallas_call(
        functools.partial(pair_body, link),
        out_shape=[struct((span, lines), F32)] + [struct((span, lines), link)] * (owners - 1),
        in_specs=[VMEM] * 2,
        out_specs=[VMEM] * owners,
        compiler_params=params(COEF * lines * 8 + 4 * MIB),
        name="pair",
    )(mine, other)
    pieces = [sums[0]] + [swap(sums[k], "rot", owners, k) for k in range(1, owners)]
    coefficients = pl.pallas_call(
        last_body,
        out_shape=struct((lines, span), F32),
        in_specs=[VMEM] * owners,
        out_specs=VMEM,
        compiler_params=params(COEF * lines * 4 + 4 * MIB),
        name="last",
    )(*pieces)
    coefficients = jnp.transpose(coefficients.reshape(parts, shells_here, span), (2, 0, 1))
    return coefficients, evidence.reshape(images_here)


def solution(mesh):
    in_specs = (
        P(None, "shell", "ang", ("grp", "rot")),
        P(None, "shell", "ang", ("grp", "rot")),
        P(("grp", "shell")),
        P(None, ("grp", "rot")),
        P(("grp", "rot"), None),
        P(("grp", "rot"), None, None),
        P(("grp", "rot")),
    )
    out_specs = (P(("grp", "rot", "ang"), None, "shell"), P(("grp", "rot")))
    return jax.shard_map(
        per_device, mesh=mesh, in_specs=in_specs, out_specs=out_specs, check_vma=False
    )
```

```python
import functools
import math

import jax
import jax.numpy as jnp
from jax import lax
from jax.experimental import pallas as pl
from jax.experimental.pallas import tpu as pltpu
from jax.sharding import PartitionSpec as P

ORDER = 32
COEF = ORDER * ORDER
LANES = 128
SUBLANES = 8
TILE = SUBLANES * LANES
MIB = 1 << 20


SMEM = pl.BlockSpec(memory_space=pltpu.SMEM)
VMEM = pl.BlockSpec(memory_space=pltpu.VMEM)
HBM = pl.BlockSpec(memory_space=pltpu.HBM)
F32 = jnp.float32
BF16 = jnp.bfloat16
I32 = jnp.int32


def struct(shape, dtype):
    return jax.ShapeDtypeStruct(shape, dtype)


def iota(shape, dim):
    return lax.broadcasted_iota(I32, shape, dim)


def slot_block(count_ref, blocks, owner, position):
    found = jnp.full_like(position, -1)
    start = 0
    for block in range(blocks):
        stop = start + count_ref[block, owner]
        found = jnp.where((position >= start) & (position < stop), block, found)
        start = stop
    return found


def stage_body(reference_ref, angle_ref, out_ref, euler_ref, sems):
    features, rotations = reference_ref.shape
    angles = pltpu.make_async_copy(angle_ref, euler_ref, sems.at[0])
    angles.start()
    copy = pltpu.make_async_copy(reference_ref, out_ref.at[pl.ds(0, features), :], sems.at[1])
    copy.start()
    angles.wait()
    line = iota((SUBLANES, rotations), 0)
    rest = jnp.where(
        line == 0,
        euler_ref[0:1, :],
        jnp.where(line == 1, euler_ref[1:2, :], jnp.where(line == 2, euler_ref[2:3, :], 0.0)),
    )
    terms = []
    for unused in range(3):
        term = rest.astype(BF16).astype(F32)
        terms.append(term)
        rest = rest - term
    terms.append(jnp.zeros((LANES - 3 * SUBLANES, rotations), F32))
    out_ref[features:, :] = jnp.concatenate(terms, axis=0).astype(BF16)
    copy.wait()


def select_body(asked, *refs):
    request_refs = refs[:asked]
    table_ref = refs[asked]
    out_refs = refs[asked + 1 :]
    owners = len(out_refs)
    rotations = table_ref.shape[1]
    slots = out_refs[0].shape[0]
    me = lax.axis_index("rot")
    row = iota((slots, LANES), 0)
    groups = []
    for turn in range(owners):
        if asked == owners:
            blocks = request_refs[turn].shape[0]
            counts = [request_refs[turn][block, owners, me] for block in range(blocks)]
        else:
            peer = lax.bitwise_xor(me, turn)
            blocks = request_refs[0].shape[1]
            counts = [request_refs[0][peer, block, slots] for block in range(blocks)]
        group = jnp.full((slots, LANES), -1, I32)
        for position in range(slots):
            value = jnp.int32(-1)
            start = jnp.int32(0)
            for block in range(blocks):
                local = position - start
                inside = (local >= 0) & (local < counts[block])
                local = jnp.clip(local, 0, slots - 1)
                if asked == owners:
                    entry = request_refs[turn][block, me, local]
                else:
                    entry = request_refs[0][peer, block, local]
                value = jnp.where(inside, entry, value)
                start = start + counts[block]
            group = jnp.where(row == position, value, group)
        groups.append(group)
    wanted = jnp.concatenate(groups, axis=0)
    wanted = jnp.concatenate([wanted] * (rotations // LANES), axis=1)
    chosen = jnp.where(wanted == iota(wanted.shape, 1), 1.0, 0.0).astype(BF16)
    picked = lax.dot_general(
        chosen, table_ref[...], (((1,), (1,)), ((), ())), preferred_element_type=F32
    )
    for turn, out_ref in enumerate(out_refs):
        out_ref[...] = picked[turn * slots : (turn + 1) * slots].astype(BF16)


def weigh_body(angles_here, block_size, noise_ref, order_ref, *refs):
    image_refs = refs[:-3]
    natural_ref, turned_ref, block_ref = refs[-3:]
    images = natural_ref.shape[1]
    lines = natural_ref.shape[0] // angles_here
    shells = noise_ref.shape[0]
    step = pl.program_id(0)
    row = iota((lines, LANES), 0)
    column = jnp.zeros((lines, LANES), F32)
    for line in range(lines):
        weight = noise_ref[lax.rem(step * lines + line, shells)]
        column = jnp.where(row == line, weight, column)
        rows = slice(line * angles_here, (line + 1) * angles_here)
        for side, image_ref in enumerate(image_refs):
            lanes = slice(side * LANES, (side + 1) * LANES)
            natural_ref[rows, lanes] = (image_ref[rows, :] * weight).astype(BF16)
    for angle in range(angles_here):
        for side, image_ref in enumerate(image_refs):
            lanes = slice(side * LANES, (side + 1) * LANES)
            plane = image_ref[pl.ds(angle, lines, stride=angles_here), :]
            turned_ref[angle, :, lanes] = (plane * column).astype(BF16)

    @pl.when(step == 0)
    def find_blocks():
        same = jnp.where(order_ref[...] == iota((images, images), 0), 1.0, 0.0).astype(BF16)
        block_of = (iota((SUBLANES, images), 1) // block_size).astype(F32).astype(BF16)
        block_ref[...] = lax.dot_general(
            block_of, same, (((1,), (1,)), ((), ())), preferred_element_type=F32
        )


def score_body(noise_ref, natural_ref, *refs):
    slice_refs = refs[:-2]
    score_ref, euler_ref = refs[-2:]
    features = natural_ref.shape[0]
    slices = jnp.concatenate([ref[:, :features].astype(F32) for ref in slice_refs], axis=0)
    norms = jnp.sum(slices * slices * noise_ref[...], axis=1, keepdims=True)
    products = jnp.dot(slices.astype(BF16), natural_ref[...], preferred_element_type=F32)
    score_ref[...] = 2.0 * products - norms
    terms = jnp.concatenate([ref[:, features:].astype(F32) for ref in slice_refs], axis=0)
    slots = terms.shape[0]
    terms = terms.astype(BF16)
    repeats = max(1, slots // LANES)
    line = iota((SUBLANES, LANES), 0)
    planes = [jnp.zeros((SUBLANES, LANES), F32)] * 3
    for repeat in range(repeats):
        place = lax.rem(repeat * LANES + iota((slots, LANES), 1), slots)
        spread = jnp.where(place == iota((slots, LANES), 0), 1.0, 0.0).astype(BF16)
        rows = lax.dot_general(
            terms, spread, (((0,), (0,)), ((), ())), preferred_element_type=F32
        )
        whole = rows[:8] + rows[8:16] + rows[16:24]
        here = lax.rem(line, repeats) == repeat
        planes = [
            jnp.where(here, whole[axis : axis + 1, :], planes[axis]) for axis in range(3)
        ]
    for axis in range(3):
        euler_ref[axis] = planes[axis]


def harmonic_constants():
    first = {}
    second = {}
    for degree in range(ORDER):
        for azimuth in range(degree):
            first[degree, azimuth] = math.sqrt(
                (4.0 * degree * degree - 1.0) / (degree * degree - azimuth * azimuth)
            )
            lower = max((degree - 1.0) ** 2 - azimuth * azimuth, 0.0)
            second[degree, azimuth] = math.sqrt(lower / max(4.0 * (degree - 1.0) ** 2 - 1.0, 1.0))
    diagonal = []
    running = 1.0
    for degree in range(ORDER):
        if degree > 0:
            running = running * (2.0 * degree - 1.0) / (2.0 * degree)
        diagonal.append(math.sqrt((2.0 * degree + 1.0) / (4.0 * math.pi) * running))
    return first, second, diagonal


def harmonic_body(slots, angles_here, angle_count, euler_ref, out_ref, rows_ref):
    first, second, diagonal = harmonic_constants()
    tile = (SUBLANES, LANES)
    column = pl.program_id(0) * TILE + iota(tile, 0) * LANES + iota(tile, 1)
    angle = lax.axis_index("ang") * angles_here + column // slots
    phase = 2.0 * math.pi / angle_count * angle.astype(F32) + euler_ref[2]
    cos_phase = jnp.cos(phase)
    sin_phase = jnp.sin(phase)
    cos_alpha = jnp.cos(euler_ref[0])
    sin_alpha = jnp.sin(euler_ref[0])
    cos_beta = jnp.cos(euler_ref[1])
    sin_beta = jnp.sin(euler_ref[1])
    along_x = cos_alpha * cos_beta * cos_phase - sin_alpha * sin_phase
    along_y = sin_alpha * cos_beta * cos_phase + cos_alpha * sin_phase
    along_z = -sin_beta * cos_phase

    def put(index, value):
        rows_ref[index * SUBLANES : (index + 1) * SUBLANES, :] = value

    real_part = jnp.ones(tile, F32)
    imag_part = jnp.zeros(tile, F32)
    for azimuth in range(ORDER):
        real_scaled = real_part * math.sqrt(2.0)
        imag_scaled = imag_part * math.sqrt(2.0)
        earlier = None
        current = None
        for degree in range(azimuth, ORDER):
            if degree == azimuth:
                value = jnp.full(tile, diagonal[azimuth], F32)
            elif degree == azimuth + 1:
                value = (first[degree, azimuth] * along_z) * current
            else:
                value = first[degree, azimuth] * (
                    along_z * current - second[degree, azimuth] * earlier
                )
            earlier, current = current, value
            if azimuth == 0:
                put(degree * degree, value)
            else:
                put(degree * degree + 2 * azimuth - 1, value * real_scaled)
                put(degree * degree + 2 * azimuth, value * imag_scaled)
        real_part, imag_part = (
            along_x * real_part - along_y * imag_part,
            along_x * imag_part + along_y * real_part,
        )
    for part in range(SUBLANES):
        out_ref[:, part * LANES : (part + 1) * LANES] = rows_ref[
            pl.ds(part, COEF, stride=SUBLANES), :
        ].astype(BF16)


def finish_body(
    angles_here, count_ref, block_ref, turned_ref, harmonic_ref, *refs
):
    blocks, owners = count_ref.shape
    evidence_ref, mine_ref, theirs_ref, average_ref, coef_ref = refs[-5:]
    sums = [ref[...] for ref in refs[:-5]]
    while len(sums) > 1:
        sums = [sums[i] + sums[i + 1] for i in range(0, len(sums), 2)]
    scores = sums[0]
    total, images = scores.shape
    slots = total // owners
    me = lax.axis_index("rot")
    ang = lax.axis_index("ang")
    position = iota((slots, images), 0)
    groups = []
    for turn in range(owners):
        groups.append(slot_block(count_ref, blocks, lax.bitwise_xor(me, turn), position))
    owner_block = jnp.concatenate(groups, axis=0).astype(F32)
    valid = owner_block == block_ref[0:1, :]
    masked = jnp.where(valid, scores, -jnp.inf)
    highest = jnp.max(masked, axis=0, keepdims=True)
    totals = jnp.sum(jnp.exp(masked - highest), axis=0, keepdims=True)
    evidence = highest + jnp.log(totals)
    evidence_ref[...] = evidence
    weights = jnp.where(valid, jnp.exp(masked - evidence), 0.0).astype(BF16)
    averages = lax.dot_general(
        weights, turned_ref[...], (((1,), (1,)), ((), ())), preferred_element_type=F32
    ).astype(BF16)
    lines = turned_ref.shape[0] // angles_here
    for angle in range(angles_here):
        average_ref[angle * total : (angle + 1) * total, :] = averages[
            :, angle * lines : (angle + 1) * lines
        ]
    coef_ref[...] = jnp.dot(harmonic_ref[...], average_ref[...], preferred_element_type=F32)
    parts = coef_ref.shape[0] // (owners * mine_ref.shape[1])
    span = mine_ref.shape[1]
    for turn in range(owners):
        owner = lax.bitwise_xor(me, turn)
        here = pl.multiple_of((owner * parts + ang) * span, span)
        there = pl.multiple_of((owner * parts + (parts - 1 - ang)) * span, span)
        mine_ref[turn] = coef_ref[pl.ds(here, span), :]
        theirs_ref[turn] = coef_ref[pl.ds(there, span), :]


def pair_body(link, mine_ref, other_ref, *out_refs):
    for turn, out_ref in enumerate(out_refs):
        out_ref[...] = (mine_ref[turn] + other_ref[turn]).astype(out_ref.dtype)


def last_body(*refs):
    out_ref = refs[-1]
    total = refs[0][...]
    for ref in refs[1:-1]:
        total = total + ref[...].astype(F32)
    out_ref[...] = total.T


def block_at(side, step):
    return step, side


def params(limit, **more):
    return pltpu.CompilerParams(vmem_limit_bytes=int(min(limit, 60 * MIB)), **more)


def in_hbm(array):
    return pltpu.with_memory_space_constraint(array, pltpu.HBM)


def swap(array, axis, size, turn):
    return lax.ppermute(array, axis, [(i, i ^ turn) for i in range(size)])


def per_device(
    images, references, noise_weight, euler_angles, candidate_count, candidate_rotation, image_order
):
    owners = lax.axis_size("rot")
    angle_parts = lax.axis_size("ang")
    shell_parts = lax.axis_size("shell")
    parts, shells_here, angles_here, images_here = images.shape
    lines = parts * shells_here
    features = lines * angles_here
    rotations_here = references.shape[3]
    blocks_here, unused, slots = candidate_rotation.shape
    total = owners * slots
    wide = features + LANES
    columns = angles_here * total
    span = COEF // (owners * angle_parts)
    link = BF16

    if owners <= SUBLANES:
        request = jnp.concatenate(
            [
                candidate_rotation,
                jnp.pad(candidate_count[:, None, :], ((0, 0), (0, 0), (0, slots - owners))),
            ],
            axis=1,
        )
        requests = [request] + [swap(request, "rot", owners, k) for k in range(1, owners)]
    else:
        request = jnp.concatenate([candidate_rotation, candidate_count[:, :, None]], axis=2)
        requests = [lax.all_to_all(jnp.swapaxes(request, 0, 1), "rot", 0, 0, tiled=True)]
    table = pl.pallas_call(
        stage_body,
        out_shape=struct((wide, rotations_here), BF16),
        in_specs=[HBM, HBM],
        out_specs=VMEM,
        scratch_shapes=[
            pltpu.VMEM((3, rotations_here), F32),
            pltpu.SemaphoreType.DMA((2,)),
        ],
        cost_estimate=pl.CostEstimate(
            flops=wide * rotations_here, bytes_accessed=4 * wide * rotations_here, transcendentals=0
        ),
        compiler_params=params(wide * rotations_here * 2 + 2 * MIB),
        name="stage",
    )(in_hbm(references.reshape(features, rotations_here)), in_hbm(euler_angles))
    chosen = pl.pallas_call(
        functools.partial(select_body, len(requests)),
        out_shape=[struct((slots, wide), BF16)] * owners,
        in_specs=[SMEM] * len(requests) + [VMEM],
        out_specs=[VMEM] * owners,
        compiler_params=params(wide * rotations_here * 2 + total * wide * 8 + 4 * MIB),
        name="select",
    )(*requests, table)
    slices = [chosen[0]] + [swap(chosen[k], "rot", owners, k) for k in range(1, owners)]

    chunk = 16
    image_table = in_hbm(images.reshape(features, images_here))
    sides = images_here // LANES
    natural, turned, image_block = pl.pallas_call(
        functools.partial(weigh_body, angles_here, images_here // blocks_here),
        grid=(lines // chunk,),
        out_shape=[
            struct((features, images_here), BF16),
            struct((angles_here, lines, images_here), BF16),
            struct((SUBLANES, images_here), F32),
        ],
        in_specs=[
            SMEM,
            pl.BlockSpec((1, images_here), lambda i: (0, 0)),
        ]
        + [
            pl.BlockSpec((chunk * angles_here, LANES), functools.partial(block_at, side))
            for side in range(sides)
        ],
        out_specs=[
            pl.BlockSpec((chunk * angles_here, images_here), lambda i: (i, 0)),
            pl.BlockSpec((angles_here, chunk, images_here), lambda i: (0, i, 0)),
            pl.BlockSpec((SUBLANES, images_here), lambda i: (0, 0)),
        ],
        cost_estimate=pl.CostEstimate(
            flops=4 * features * images_here, bytes_accessed=8 * features * images_here, transcendentals=0
        ),
        compiler_params=params(8 * chunk * angles_here * images_here * 4),
        name="weigh",
    )(noise_weight, image_order[None], *[image_table] * sides)

    noise_row = jnp.broadcast_to(
        noise_weight[None, :, None], (parts, shells_here, angles_here)
    ).reshape(1, features)
    partial, eulers = pl.pallas_call(
        score_body,
        out_shape=[struct((total, images_here), F32), struct((3, SUBLANES, LANES), F32)],
        in_specs=[VMEM] * (2 + owners),
        out_specs=[VMEM] * 2,
        compiler_params=params(features * images_here * 2 + total * wide * 12 + 4 * MIB),
        name="score",
    )(noise_row, natural, *slices)

    count = shell_parts * angle_parts
    shares = [partial] + [
        lax.ppermute(partial, ("shell", "ang"), [(i, i ^ k) for i in range(count)])
        for k in range(1, count)
    ]

    harmonics = pl.pallas_call(
        functools.partial(harmonic_body, total, angles_here, angles_here * angle_parts),
        grid=(columns // TILE,),
        out_shape=struct((COEF, columns), BF16),
        in_specs=[pl.BlockSpec((3, SUBLANES, LANES), lambda i: (0, 0, 0))],
        out_specs=pl.BlockSpec((COEF, TILE), lambda i: (0, i)),
        scratch_shapes=[pltpu.VMEM((COEF * SUBLANES, LANES), F32)],
        cost_estimate=pl.CostEstimate(
            flops=8 * COEF * columns, bytes_accessed=2 * COEF * columns, transcendentals=6 * columns
        ),
        compiler_params=params(12 * MIB),
        name="harmonics",
    )(eulers)

    evidence, mine, theirs = pl.pallas_call(
        functools.partial(finish_body, angles_here),
        out_shape=[
            struct((1, images_here), F32),
            struct((owners, span, lines), F32),
            struct((owners, span, lines), F32),
        ],
        in_specs=[SMEM] + [VMEM] * (3 + count),
        out_specs=[VMEM] * 3,
        scratch_shapes=[pltpu.VMEM((columns, lines), BF16), pltpu.VMEM((COEF, lines), F32)],
        compiler_params=params(
            features * images_here * 2 + COEF * columns * 2 + total * features * 8
            + columns * lines * 4 + COEF * lines * 16 + 4 * MIB
        ),
        name="finish",
    )(candidate_count, image_block, turned.reshape(features, images_here), harmonics, *shares)

    other = swap(theirs, "ang", angle_parts, 1)
    sums = pl.pallas_call(
        functools.partial(pair_body, link),
        out_shape=[struct((span, lines), F32)] + [struct((span, lines), link)] * (owners - 1),
        in_specs=[VMEM] * 2,
        out_specs=[VMEM] * owners,
        compiler_params=params(COEF * lines * 8 + 4 * MIB),
        name="pair",
    )(mine, other)
    pieces = [sums[0]] + [swap(sums[k], "rot", owners, k) for k in range(1, owners)]
    coefficients = pl.pallas_call(
        last_body,
        out_shape=struct((lines, span), F32),
        in_specs=[VMEM] * owners,
        out_specs=VMEM,
        compiler_params=params(COEF * lines * 4 + 4 * MIB),
        name="last",
    )(*pieces)
    coefficients = jnp.transpose(coefficients.reshape(parts, shells_here, span), (2, 0, 1))
    return coefficients, evidence.reshape(images_here)


def solution(mesh):
    in_specs = (
        P(None, "shell", "ang", ("grp", "rot")),
        P(None, "shell", "ang", ("grp", "rot")),
        P(("grp", "shell")),
        P(None, ("grp", "rot")),
        P(("grp", "rot"), None),
        P(("grp", "rot"), None, None),
        P(("grp", "rot")),
    )
    out_specs = (P(("grp", "rot", "ang"), None, "shell"), P(("grp", "rot")))
    return jax.shard_map(
        per_device, mesh=mesh, in_specs=in_specs, out_specs=out_specs, check_vma=False
    )
```

```python
import functools
import math

import jax
import jax.numpy as jnp
from jax import lax
from jax.experimental import pallas as pl
from jax.experimental.pallas import tpu as pltpu
from jax.sharding import PartitionSpec as P

ORDER = 32
COEF = ORDER * ORDER
LANES = 128
SUBLANES = 8
TILE = SUBLANES * LANES
MIB = 1 << 20


SMEM = pl.BlockSpec(memory_space=pltpu.SMEM)
VMEM = pl.BlockSpec(memory_space=pltpu.VMEM)
HBM = pl.BlockSpec(memory_space=pltpu.HBM)
F32 = jnp.float32
BF16 = jnp.bfloat16
I32 = jnp.int32


def struct(shape, dtype):
    return jax.ShapeDtypeStruct(shape, dtype)


def iota(shape, dim):
    return lax.broadcasted_iota(I32, shape, dim)


def stage_body(
    block_size, reference_ref, angle_ref, order_ref, count_ref, table_ref, mask_ref,
    euler_here, order_here, count_here, sems
):
    features, rotations = reference_ref.shape
    small = [
        pltpu.make_async_copy(angle_ref, euler_here, sems.at[0]),
        pltpu.make_async_copy(order_ref, order_here, sems.at[1]),
        pltpu.make_async_copy(count_ref, count_here, sems.at[2]),
    ]
    for copy in small:
        copy.start()
    large = pltpu.make_async_copy(reference_ref, table_ref.at[pl.ds(0, features), :], sems.at[3])
    large.start()
    for copy in small:
        copy.wait()
    line = iota((SUBLANES, rotations), 0)
    rest = jnp.where(
        line == 0,
        euler_here[0:1, :],
        jnp.where(line == 1, euler_here[1:2, :], jnp.where(line == 2, euler_here[2:3, :], 0.0)),
    )
    terms = []
    for unused in range(3):
        term = rest.astype(BF16).astype(F32)
        terms.append(term)
        rest = rest - term
    terms.append(jnp.zeros((LANES - 3 * SUBLANES, rotations), F32))
    table_ref[features:, :] = jnp.concatenate(terms, axis=0).astype(BF16)

    images = order_here.shape[1]
    same = jnp.where(order_here[...] == iota((images, images), 0), 1.0, 0.0).astype(BF16)
    block_of = (iota((SUBLANES, images), 1) // block_size).astype(F32).astype(BF16)
    image_block = lax.dot_general(
        block_of, same, (((1,), (1,)), ((), ())), preferred_element_type=F32
    )[0:1, :]
    blocks, owners = count_here.shape
    slots = mask_ref.shape[0] // owners
    me = lax.axis_index("rot")
    position = iota((slots, images), 0).astype(F32)
    counts = count_here[...].astype(F32)
    lane = iota((blocks, owners), 1)
    for turn in range(owners):
        listed = jnp.sum(
            jnp.where(lane == lax.bitwise_xor(me, turn), counts, 0.0), axis=1, keepdims=True
        )
        mask = jnp.full((slots, images), -jnp.inf, F32)
        start = jnp.zeros((1, 1), F32)
        for block in range(blocks):
            stop = start + listed[block : block + 1, :]
            inside = (position >= start) & (position < stop) & (image_block == block)
            mask = jnp.where(inside, 0.0, mask)
            start = stop
        mask_ref[turn * slots : (turn + 1) * slots, :] = mask
    large.wait()


def select_body(asked, *refs):
    request_refs = refs[:asked]
    table_ref = refs[asked]
    out_refs = refs[asked + 1 :]
    owners = len(out_refs)
    rotations = table_ref.shape[1]
    slots = out_refs[0].shape[0]
    me = lax.axis_index("rot")
    direct = asked == owners
    blocks = request_refs[0].shape[0 if direct else 1]
    rows = []
    counts = []
    for turn in range(owners):
        for block in range(blocks):
            if direct:
                rows.append(request_refs[turn][block, pl.ds(me, 1), :])
                counts.append(request_refs[turn][block, owners : owners + 1, :])
            else:
                both = request_refs[0][lax.bitwise_xor(me, turn), block : block + 1, :]
                rows.append(both[:, :slots])
                counts.append(both[:, slots:])
    counts = jnp.concatenate(counts, axis=0).astype(F32)
    if direct:
        counts = jnp.sum(jnp.where(iota(counts.shape, 1) == me, counts, 0.0), axis=1, keepdims=True)
    to = iota((slots, slots), 0).astype(F32)
    entry = iota((slots, slots), 1).astype(F32)
    groups = []
    for turn in range(owners):
        group = jnp.zeros((slots, slots), F32)
        start = jnp.zeros((1, 1), F32)
        for block in range(blocks):
            place = turn * blocks + block
            count = counts[place : place + 1, :]
            inside = (to == entry + start) & (entry < count)
            group = group + jnp.where(inside, rows[place].astype(F32) + 1.0, 0.0)
            start = start + count
        groups.append(group)
    wanted = jnp.sum(jnp.concatenate(groups, axis=0), axis=1, keepdims=True)
    lane = iota((owners * slots, rotations), 1).astype(F32) + 1.0
    chosen = jnp.where(wanted == lane, 1.0, 0.0).astype(BF16)
    picked = lax.dot_general(
        chosen, table_ref[...], (((1,), (1,)), ((), ())), preferred_element_type=F32
    )
    for turn, out_ref in enumerate(out_refs):
        out_ref[...] = picked[turn * slots : (turn + 1) * slots].astype(BF16)


def weigh_body(angles_here, chunk, noise_ref, image_ref, natural_ref, turned_ref, held_ref, sems):
    features, images = image_ref.shape
    shells = noise_ref.shape[0]
    size = chunk * angles_here
    steps = features // size

    def copy(step):
        rows = pl.ds(pl.multiple_of(step * size, size), size)
        return pltpu.make_async_copy(image_ref.at[rows, :], held_ref.at[rows, :], sems.at[step])

    for step in range(steps):
        copy(step).start()

    def one_chunk(step, carry):
        copy(step).wait()
        for side in range(images // LANES):
            lanes = slice(side * LANES, (side + 1) * LANES)
            planes = []
            for line in range(chunk):
                weight = noise_ref[lax.rem(step * chunk + line, shells)]
                rows = pl.ds(
                    pl.multiple_of((step * chunk + line) * angles_here, angles_here), angles_here
                )
                plane = held_ref[rows, lanes] * weight
                natural_ref[rows, lanes] = plane.astype(BF16)
                planes.append(plane)
            turned_ref[:, pl.ds(pl.multiple_of(step * chunk, chunk), chunk), lanes] = jnp.swapaxes(
                jnp.stack(planes, axis=0), 0, 1
            ).astype(BF16)
        return carry

    lax.fori_loop(0, steps, one_chunk, 0)


def score_body(noise_ref, natural_ref, *refs):
    slice_refs = refs[:-2]
    score_ref, euler_ref = refs[-2:]
    features = natural_ref.shape[0]
    slices = jnp.concatenate([ref[:, :features].astype(F32) for ref in slice_refs], axis=0)
    norms = jnp.sum(slices * slices * noise_ref[...], axis=1, keepdims=True)
    products = jnp.dot(slices.astype(BF16), natural_ref[...], preferred_element_type=F32)
    score_ref[...] = 2.0 * products - norms
    terms = jnp.concatenate([ref[:, features:].astype(F32) for ref in slice_refs], axis=0)
    slots = terms.shape[0]
    terms = terms.astype(BF16)
    repeats = max(1, slots // LANES)
    line = iota((SUBLANES, LANES), 0)
    planes = [jnp.zeros((SUBLANES, LANES), F32)] * 3
    for repeat in range(repeats):
        place = lax.rem(repeat * LANES + iota((slots, LANES), 1), slots)
        spread = jnp.where(place == iota((slots, LANES), 0), 1.0, 0.0).astype(BF16)
        rows = lax.dot_general(
            terms, spread, (((0,), (0,)), ((), ())), preferred_element_type=F32
        )
        whole = rows[:8] + rows[8:16] + rows[16:24]
        here = lax.rem(line, repeats) == repeat
        planes = [
            jnp.where(here, whole[axis : axis + 1, :], planes[axis]) for axis in range(3)
        ]
    for axis in range(3):
        euler_ref[axis] = planes[axis]


def harmonic_constants():
    first = {}
    second = {}
    for degree in range(ORDER):
        for azimuth in range(degree):
            first[degree, azimuth] = math.sqrt(
                (4.0 * degree * degree - 1.0) / (degree * degree - azimuth * azimuth)
            )
            lower = max((degree - 1.0) ** 2 - azimuth * azimuth, 0.0)
            second[degree, azimuth] = math.sqrt(lower / max(4.0 * (degree - 1.0) ** 2 - 1.0, 1.0))
    diagonal = []
    running = 1.0
    for degree in range(ORDER):
        if degree > 0:
            running = running * (2.0 * degree - 1.0) / (2.0 * degree)
        diagonal.append(math.sqrt((2.0 * degree + 1.0) / (4.0 * math.pi) * running))
    return first, second, diagonal


def harmonic_body(slots, angles_here, owners, angle_parts, euler_ref, out_ref, rows_ref):
    first, second, diagonal = harmonic_constants()
    tile = (SUBLANES, LANES)
    column = pl.program_id(0) * TILE + iota(tile, 0) * LANES + iota(tile, 1)
    angle = lax.axis_index("ang") * angles_here + column // slots
    phase = 2.0 * math.pi / (angles_here * angle_parts) * angle.astype(F32) + euler_ref[2]
    cos_phase = jnp.cos(phase)
    sin_phase = jnp.sin(phase)
    cos_alpha = jnp.cos(euler_ref[0])
    sin_alpha = jnp.sin(euler_ref[0])
    cos_beta = jnp.cos(euler_ref[1])
    sin_beta = jnp.sin(euler_ref[1])
    along_x = cos_alpha * cos_beta * cos_phase - sin_alpha * sin_phase
    along_y = sin_alpha * cos_beta * cos_phase + cos_alpha * sin_phase
    along_z = -sin_beta * cos_phase

    def put(index, value):
        rows_ref[index * SUBLANES : (index + 1) * SUBLANES, :] = value

    real_part = jnp.ones(tile, F32)
    imag_part = jnp.zeros(tile, F32)
    for azimuth in range(ORDER):
        real_scaled = real_part * math.sqrt(2.0)
        imag_scaled = imag_part * math.sqrt(2.0)
        earlier = None
        current = None
        for degree in range(azimuth, ORDER):
            if degree == azimuth:
                value = jnp.full(tile, diagonal[azimuth], F32)
            elif degree == azimuth + 1:
                value = (first[degree, azimuth] * along_z) * current
            else:
                value = first[degree, azimuth] * (
                    along_z * current - second[degree, azimuth] * earlier
                )
            earlier, current = current, value
            if azimuth == 0:
                put(degree * degree, value)
            else:
                put(degree * degree + 2 * azimuth - 1, value * real_scaled)
                put(degree * degree + 2 * azimuth, value * imag_scaled)
        real_part, imag_part = (
            along_x * real_part - along_y * imag_part,
            along_x * imag_part + along_y * real_part,
        )
    me = lax.axis_index("rot")
    here = lax.axis_index("ang")
    span = COEF // (owners * angle_parts)
    for owner in range(owners):
        for ang in range(angle_parts):
            side = lax.rem(here + ang, angle_parts)
            place = (side * owners + lax.bitwise_xor(me, owner)) * span
            rows = pl.ds(pl.multiple_of(place, span), span)
            start = (owner * angle_parts + ang) * span * SUBLANES
            for part in range(SUBLANES):
                out_ref[rows, part * LANES : (part + 1) * LANES] = rows_ref[
                    pl.ds(start + part, span, stride=SUBLANES), :
                ].astype(BF16)


def finish_body(angles_here, mask_ref, turned_ref, harmonic_ref, *refs):
    evidence_ref, mine_ref, theirs_ref, average_ref = refs[-4:]
    sums = [ref[...] for ref in refs[:-4]]
    while len(sums) > 1:
        sums = [sums[i] + sums[i + 1] for i in range(0, len(sums), 2)]
    masked = sums[0] + mask_ref[...]
    total = masked.shape[0]
    highest = jnp.max(masked, axis=0, keepdims=True)
    shares = jnp.exp(masked - highest)
    totals = jnp.sum(shares, axis=0, keepdims=True)
    weights = (shares / totals).astype(BF16)
    averages = lax.dot_general(
        weights, turned_ref[...], (((1,), (1,)), ((), ())), preferred_element_type=F32
    ).astype(BF16)
    evidence_ref[...] = highest + jnp.log(totals)
    lines = turned_ref.shape[0] // angles_here
    for angle in range(angles_here):
        average_ref[angle * total : (angle + 1) * total, :] = averages[
            :, angle * lines : (angle + 1) * lines
        ]
    kept = mine_ref.shape[0] * mine_ref.shape[1]
    for out_ref, first in ((theirs_ref, kept), (mine_ref, 0)):
        out_ref[...] = jnp.dot(
            harmonic_ref[first : first + kept, :], average_ref[...], preferred_element_type=F32
        ).reshape(out_ref.shape)


def pair_body(link, mine_ref, other_ref, *out_refs):
    for turn, out_ref in enumerate(out_refs):
        out_ref[...] = (mine_ref[turn] + other_ref[turn]).astype(out_ref.dtype)


def last_body(*refs):
    out_ref = refs[-1]
    total = refs[0][...]
    for ref in refs[1:-1]:
        total = total + ref[...].astype(F32)
    out_ref[...] = total.T


def params(limit, **more):
    return pltpu.CompilerParams(vmem_limit_bytes=int(min(limit, 60 * MIB)), **more)


def in_hbm(array):
    return pltpu.with_memory_space_constraint(array, pltpu.HBM)


def swap(array, axis, size, turn):
    return lax.ppermute(array, axis, [(i, i ^ turn) for i in range(size)])


def per_device(
    images, references, noise_weight, euler_angles, candidate_count, candidate_rotation, image_order
):
    owners = lax.axis_size("rot")
    angle_parts = lax.axis_size("ang")
    shell_parts = lax.axis_size("shell")
    parts, shells_here, angles_here, images_here = images.shape
    lines = parts * shells_here
    features = lines * angles_here
    rotations_here = references.shape[3]
    blocks_here, unused, slots = candidate_rotation.shape
    total = owners * slots
    wide = features + LANES
    columns = angles_here * total
    span = COEF // (owners * angle_parts)
    link = BF16

    if owners <= SUBLANES:
        request = jnp.concatenate(
            [
                candidate_rotation,
                jnp.pad(candidate_count[:, None, :], ((0, 0), (0, 0), (0, slots - owners))),
            ],
            axis=1,
        )
        requests = [request] + [swap(request, "rot", owners, k) for k in range(1, owners)]
    else:
        request = jnp.concatenate([candidate_rotation, candidate_count[:, :, None]], axis=2)
        requests = [lax.all_to_all(jnp.swapaxes(request, 0, 1), "rot", 0, 0, tiled=True)]
    table, mask = pl.pallas_call(
        functools.partial(stage_body, images_here // blocks_here),
        out_shape=[struct((wide, rotations_here), BF16), struct((total, images_here), F32)],
        in_specs=[HBM] * 4,
        out_specs=[VMEM] * 2,
        scratch_shapes=[
            pltpu.VMEM((3, rotations_here), F32),
            pltpu.VMEM((1, images_here), I32),
            pltpu.VMEM((blocks_here, owners), I32),
            pltpu.SemaphoreType.DMA((4,)),
        ],
        cost_estimate=pl.CostEstimate(
            flops=wide * rotations_here, bytes_accessed=4 * wide * rotations_here, transcendentals=0
        ),
        compiler_params=params(wide * rotations_here * 2 + total * images_here * 8 + 4 * MIB),
        name="stage",
    )(
        in_hbm(references.reshape(features, rotations_here)),
        in_hbm(euler_angles),
        in_hbm(image_order[None]),
        in_hbm(candidate_count),
    )
    chosen = pl.pallas_call(
        functools.partial(select_body, len(requests)),
        out_shape=[struct((slots, wide), BF16)] * owners,
        in_specs=[VMEM] * (len(requests) + 1),
        out_specs=[VMEM] * owners,
        compiler_params=params(wide * rotations_here * 2 + total * wide * 8 + 4 * MIB),
        name="select",
    )(*requests, table)
    slices = [chosen[0]] + [swap(chosen[k], "rot", owners, k) for k in range(1, owners)]

    chunk = 16
    natural, turned = pl.pallas_call(
        functools.partial(weigh_body, angles_here, chunk),
        out_shape=[
            struct((features, images_here), BF16),
            struct((angles_here, lines, images_here), BF16),
        ],
        in_specs=[SMEM, HBM],
        out_specs=[VMEM] * 2,
        scratch_shapes=[
            pltpu.VMEM((features, images_here), F32),
            pltpu.SemaphoreType.DMA((lines // chunk,)),
        ],
        cost_estimate=pl.CostEstimate(
            flops=4 * features * images_here, bytes_accessed=8 * features * images_here, transcendentals=0
        ),
        compiler_params=params(features * images_here * 8 + 4 * MIB),
        name="weigh",
    )(noise_weight, in_hbm(images.reshape(features, images_here)))

    noise_row = jnp.broadcast_to(
        noise_weight[None, :, None], (parts, shells_here, angles_here)
    ).reshape(1, features)
    partial, eulers = pl.pallas_call(
        score_body,
        out_shape=[struct((total, images_here), F32), struct((3, SUBLANES, LANES), F32)],
        in_specs=[VMEM] * (2 + owners),
        out_specs=[VMEM] * 2,
        compiler_params=params(features * images_here * 2 + total * wide * 12 + 4 * MIB),
        name="score",
    )(noise_row, natural, *slices)

    count = shell_parts * angle_parts
    shares = [partial] + [
        lax.ppermute(partial, ("shell", "ang"), [(i, i ^ k) for i in range(count)])
        for k in range(1, count)
    ]

    harmonics = pl.pallas_call(
        functools.partial(harmonic_body, total, angles_here, owners, angle_parts),
        grid=(columns // TILE,),
        out_shape=struct((COEF, columns), BF16),
        in_specs=[pl.BlockSpec((3, SUBLANES, LANES), lambda i: (0, 0, 0))],
        out_specs=pl.BlockSpec((COEF, TILE), lambda i: (0, i)),
        scratch_shapes=[pltpu.VMEM((COEF * SUBLANES, LANES), F32)],
        cost_estimate=pl.CostEstimate(
            flops=8 * COEF * columns, bytes_accessed=2 * COEF * columns, transcendentals=6 * columns
        ),
        compiler_params=params(12 * MIB),
        name="harmonics",
    )(eulers)

    evidence, mine, theirs = pl.pallas_call(
        functools.partial(finish_body, angles_here),
        out_shape=[
            struct((1, images_here), F32),
            struct((owners, span, lines), F32),
            struct((owners, span, lines), F32),
        ],
        in_specs=[VMEM] * (3 + count),
        out_specs=[VMEM] * 3,
        scratch_shapes=[pltpu.VMEM((columns, lines), BF16)],
        compiler_params=params(
            features * images_here * 2 + COEF * columns * 2 + total * features * 8
            + columns * lines * 4 + COEF * lines * 16 + 4 * MIB
        ),
        name="finish",
    )(mask, turned.reshape(features, images_here), harmonics, *shares)

    other = swap(theirs, "ang", angle_parts, 1)
    sums = pl.pallas_call(
        functools.partial(pair_body, link),
        out_shape=[struct((span, lines), F32)] + [struct((span, lines), link)] * (owners - 1),
        in_specs=[VMEM] * 2,
        out_specs=[VMEM] * owners,
        compiler_params=params(COEF * lines * 8 + 4 * MIB),
        name="pair",
    )(mine, other)
    pieces = [sums[0]] + [swap(sums[k], "rot", owners, k) for k in range(1, owners)]
    coefficients = pl.pallas_call(
        last_body,
        out_shape=struct((lines, span), F32),
        in_specs=[VMEM] * owners,
        out_specs=VMEM,
        compiler_params=params(COEF * lines * 4 + 4 * MIB),
        name="last",
    )(*pieces)
    coefficients = jnp.transpose(coefficients.reshape(parts, shells_here, span), (2, 0, 1))
    return coefficients, evidence.reshape(images_here)


def solution(mesh):
    in_specs = (
        P(None, "shell", "ang", ("grp", "rot")),
        P(None, "shell", "ang", ("grp", "rot")),
        P(("grp", "shell")),
        P(None, ("grp", "rot")),
        P(("grp", "rot"), None),
        P(("grp", "rot"), None, None),
        P(("grp", "rot")),
    )
    out_specs = (P(("grp", "rot", "ang"), None, "shell"), P(("grp", "rot")))
    return jax.shard_map(
        per_device, mesh=mesh, in_specs=in_specs, out_specs=out_specs, check_vma=False
    )
```

```python
import functools
import math

import jax
import jax.numpy as jnp
from jax import lax
from jax.experimental import pallas as pl
from jax.experimental.pallas import tpu as pltpu
from jax.sharding import PartitionSpec as P


ORDER = 32
COEF = ORDER * ORDER
LANES = 128
SUBLANES = 8
TILE = SUBLANES * LANES
MIB = 1 << 20
STAGES = 8
STAGED = False


SMEM = pl.BlockSpec(memory_space=pltpu.SMEM)
VMEM = pl.BlockSpec(memory_space=pltpu.VMEM)
HBM = pl.BlockSpec(memory_space=pltpu.HBM)
F32 = jnp.float32
BF16 = jnp.bfloat16
I32 = jnp.int32


def struct(shape, dtype):
    return jax.ShapeDtypeStruct(shape, dtype)


def iota(shape, dim):
    return lax.broadcasted_iota(I32, shape, dim)


def stage_body(
    block_size, reference_ref, angle_ref, order_ref, count_ref, table_ref, mask_ref,
    euler_here, order_here, count_here, sems
):
    features, rotations = reference_ref.shape
    small = [
        pltpu.make_async_copy(angle_ref, euler_here, sems.at[0]),
        pltpu.make_async_copy(order_ref, order_here, sems.at[1]),
        pltpu.make_async_copy(count_ref, count_here, sems.at[2]),
    ]
    for copy in small:
        copy.start()
    size = features // STAGES
    large = [
        pltpu.make_async_copy(
            reference_ref.at[pl.ds(part * size, size), :],
            table_ref.at[pl.ds(part * size, size), :],
            sems.at[3 + part],
        )
        for part in range(STAGES)
    ]
    for copy in large:
        copy.start()
    for copy in small:
        copy.wait()
    line = iota((SUBLANES, rotations), 0)
    rest = jnp.where(
        line == 0,
        euler_here[0:1, :],
        jnp.where(line == 1, euler_here[1:2, :], jnp.where(line == 2, euler_here[2:3, :], 0.0)),
    )
    terms = []
    for _ in range(3):
        term = rest.astype(BF16).astype(F32)
        terms.append(term)
        rest = rest - term
    terms.append(jnp.zeros((LANES - 3 * SUBLANES, rotations), F32))
    table_ref[features:, :] = jnp.concatenate(terms, axis=0).astype(BF16)

    images = order_here.shape[1]
    same = jnp.where(order_here[...] == iota((images, images), 0), 1.0, 0.0).astype(BF16)
    block_of = (iota((SUBLANES, images), 1) // block_size).astype(F32).astype(BF16)
    image_block = lax.dot_general(
        block_of, same, (((1,), (1,)), ((), ())), preferred_element_type=F32
    )[0:1, :]
    blocks, owners = count_here.shape
    slots = mask_ref.shape[0] // owners
    me = lax.axis_index("rot")
    position = iota((slots, images), 0).astype(F32)
    counts = count_here[...].astype(F32)
    lane = iota((blocks, owners), 1)
    for turn in range(owners):
        listed = jnp.sum(
            jnp.where(lane == lax.bitwise_xor(me, turn), counts, 0.0), axis=1, keepdims=True
        )
        mask = jnp.full((slots, images), -jnp.inf, F32)
        start = jnp.zeros((1, 1), F32)
        for block in range(blocks):
            stop = start + listed[block : block + 1, :]
            inside = (position >= start) & (position < stop) & (image_block == block)
            mask = jnp.where(inside, 0.0, mask)
            start = stop
        mask_ref[turn * slots : (turn + 1) * slots, :] = mask
    for copy in large:
        copy.wait()


def select_body(asked, *refs):
    request_refs = refs[:asked]
    table_ref = refs[asked]
    out_refs = refs[asked + 1 :]
    owners = len(out_refs)
    rotations = table_ref.shape[1]
    slots = out_refs[0].shape[0]
    me = lax.axis_index("rot")
    direct = asked == owners
    blocks = request_refs[0].shape[0 if direct else 1]
    rows = []
    counts = []
    for turn in range(owners):
        for block in range(blocks):
            if direct:
                rows.append(request_refs[turn][block, pl.ds(me, 1), :])
                counts.append(request_refs[turn][block, owners : owners + 1, :])
            else:
                both = request_refs[0][lax.bitwise_xor(me, turn), block : block + 1, :]
                rows.append(both[:, :slots])
                counts.append(both[:, slots:])
    counts = jnp.concatenate(counts, axis=0).astype(F32)
    if direct:
        counts = jnp.sum(jnp.where(iota(counts.shape, 1) == me, counts, 0.0), axis=1, keepdims=True)
    to = iota((slots, slots), 0).astype(F32)
    entry = iota((slots, slots), 1).astype(F32)
    groups = []
    for turn in range(owners):
        group = jnp.zeros((slots, slots), F32)
        start = jnp.zeros((1, 1), F32)
        for block in range(blocks):
            place = turn * blocks + block
            count = counts[place : place + 1, :]
            inside = (to == entry + start) & (entry < count)
            group = group + jnp.where(inside, rows[place].astype(F32) + 1.0, 0.0)
            start = start + count
        groups.append(group)
    wanted = jnp.sum(jnp.concatenate(groups, axis=0), axis=1, keepdims=True)
    lane = iota((owners * slots, rotations), 1).astype(F32) + 1.0
    chosen = jnp.where(wanted == lane, 1.0, 0.0).astype(BF16)
    picked = lax.dot_general(
        chosen, table_ref[...], (((1,), (1,)), ((), ())), preferred_element_type=F32
    )
    for turn, out_ref in enumerate(out_refs):
        out_ref[...] = picked[turn * slots : (turn + 1) * slots].astype(BF16)


def weigh_body(angles_here, chunk, noise_ref, image_ref, natural_ref, turned_ref, held_ref, sems):
    features, images = image_ref.shape
    shells = noise_ref.shape[0]
    size = chunk * angles_here
    steps = features // size

    def copy(step):
        rows = pl.ds(pl.multiple_of(step * size, size), size)
        return pltpu.make_async_copy(image_ref.at[rows, :], held_ref.at[rows, :], sems.at[step])

    for step in range(steps):
        copy(step).start()

    def one_chunk(step, carry):
        copy(step).wait()
        for side in range(images // LANES):
            lanes = slice(side * LANES, (side + 1) * LANES)
            planes = []
            for line in range(chunk):
                weight = noise_ref[lax.rem(step * chunk + line, shells)]
                rows = pl.ds(
                    pl.multiple_of((step * chunk + line) * angles_here, angles_here), angles_here
                )
                plane = held_ref[rows, lanes] * weight
                natural_ref[rows, lanes] = plane.astype(BF16)
                planes.append(plane)
            turned_ref[:, pl.ds(pl.multiple_of(step * chunk, chunk), chunk), lanes] = jnp.swapaxes(
                jnp.stack(planes, axis=0), 0, 1
            ).astype(BF16)
        return carry

    lax.fori_loop(0, steps, one_chunk, 0)


def score_body(noise_ref, natural_ref, *refs):
    slice_refs, score_ref = refs[:-1], refs[-1]
    features = natural_ref.shape[0]
    slices = jnp.concatenate([ref[:, :features].astype(F32) for ref in slice_refs], axis=0)
    norms = jnp.sum(slices * slices * noise_ref[...], axis=1, keepdims=True)
    products = jnp.dot(slices.astype(BF16), natural_ref[...], preferred_element_type=F32)
    score_ref[...] = 2.0 * products - norms


def slot_angles(slice_refs):
    terms = jnp.concatenate([ref[:, -LANES:].astype(F32) for ref in slice_refs], axis=0)
    slots = terms.shape[0]
    terms = terms.astype(BF16)
    repeats = max(1, slots // LANES)
    line = iota((SUBLANES, LANES), 0)
    planes = [jnp.zeros((SUBLANES, LANES), F32)] * 3
    for repeat in range(repeats):
        place = lax.rem(repeat * LANES + iota((slots, LANES), 1), slots)
        spread_out = jnp.where(place == iota((slots, LANES), 0), 1.0, 0.0).astype(BF16)
        rows = lax.dot_general(
            terms, spread_out, (((0,), (0,)), ((), ())), preferred_element_type=F32
        )
        whole = rows[:8] + rows[8:16] + rows[16:24]
        here = lax.rem(line, repeats) == repeat
        planes = [
            jnp.where(here, whole[axis : axis + 1, :], planes[axis]) for axis in range(3)
        ]
    return planes


def harmonic_constants():
    first = {}
    second = {}
    for degree in range(ORDER):
        for azimuth in range(degree):
            first[degree, azimuth] = math.sqrt(
                (4.0 * degree * degree - 1.0) / (degree * degree - azimuth * azimuth)
            )
            lower = max((degree - 1.0) ** 2 - azimuth * azimuth, 0.0)
            second[degree, azimuth] = math.sqrt(lower / max(4.0 * (degree - 1.0) ** 2 - 1.0, 1.0))
    diagonal = []
    running = 1.0
    for degree in range(ORDER):
        if degree > 0:
            running = running * (2.0 * degree - 1.0) / (2.0 * degree)
        diagonal.append(math.sqrt((2.0 * degree + 1.0) / (4.0 * math.pi) * running))
    return first, second, diagonal


def harmonic_body(slots, angles_here, owners, angle_parts, *refs):
    slice_refs = refs[:-2]
    out_ref, rows_ref = refs[-2:]
    alpha, beta, gamma = slot_angles(slice_refs)
    first, second, diagonal = harmonic_constants()
    tile = (SUBLANES, LANES)
    column = pl.program_id(0) * TILE + iota(tile, 0) * LANES + iota(tile, 1)
    angle = lax.axis_index("ang") * angles_here + column // slots
    phase = 2.0 * math.pi / (angles_here * angle_parts) * angle.astype(F32) + gamma
    cos_phase = jnp.cos(phase)
    sin_phase = jnp.sin(phase)
    cos_alpha = jnp.cos(alpha)
    sin_alpha = jnp.sin(alpha)
    cos_beta = jnp.cos(beta)
    sin_beta = jnp.sin(beta)
    along_x = cos_alpha * cos_beta * cos_phase - sin_alpha * sin_phase
    along_y = sin_alpha * cos_beta * cos_phase + cos_alpha * sin_phase
    along_z = -sin_beta * cos_phase

    def put(index, value):
        rows_ref[index * SUBLANES : (index + 1) * SUBLANES, :] = value

    real_part = jnp.ones(tile, F32)
    imag_part = jnp.zeros(tile, F32)
    for azimuth in range(ORDER):
        real_scaled = real_part * math.sqrt(2.0)
        imag_scaled = imag_part * math.sqrt(2.0)
        earlier = None
        current = None
        for degree in range(azimuth, ORDER):
            if degree == azimuth:
                value = jnp.full(tile, diagonal[azimuth], F32)
            elif degree == azimuth + 1:
                value = (first[degree, azimuth] * along_z) * current
            else:
                value = first[degree, azimuth] * (
                    along_z * current - second[degree, azimuth] * earlier
                )
            earlier, current = current, value
            if azimuth == 0:
                put(degree * degree, value)
            else:
                put(degree * degree + 2 * azimuth - 1, value * real_scaled)
                put(degree * degree + 2 * azimuth, value * imag_scaled)
        real_part, imag_part = (
            along_x * real_part - along_y * imag_part,
            along_x * imag_part + along_y * real_part,
        )
    me = lax.axis_index("rot")
    here = lax.axis_index("ang")
    span = COEF // (owners * angle_parts)
    for owner in range(owners):
        for ang in range(angle_parts):
            side = lax.rem(here + ang, angle_parts)
            place = (side * owners + lax.bitwise_xor(me, owner)) * span
            rows = pl.ds(pl.multiple_of(place, span), span)
            start = (owner * angle_parts + ang) * span * SUBLANES
            for part in range(SUBLANES):
                out_ref[rows, part * LANES : (part + 1) * LANES] = rows_ref[
                    pl.ds(start + part, span, stride=SUBLANES), :
                ].astype(BF16)


def add_body(first_ref, second_ref, out_ref):
    out_ref[...] = first_ref[...] + second_ref[...]


def average_body(angles_here, mask_ref, turned_ref, harmonic_ref, *refs):
    highest_ref, totals_ref, average_ref, theirs_ref = refs[-4:]
    sums = [ref[...] for ref in refs[:-4]]
    while len(sums) > 1:
        sums = [sums[i] + sums[i + 1] for i in range(0, len(sums), 2)]
    masked = sums[0] + mask_ref[...]
    total = masked.shape[0]
    highest = jnp.max(masked, axis=0, keepdims=True)
    shares = jnp.exp(masked - highest)
    totals = jnp.sum(shares, axis=0, keepdims=True)
    weights = (shares / totals).astype(BF16)
    averages = lax.dot_general(
        weights, turned_ref[...], (((1,), (1,)), ((), ())), preferred_element_type=F32
    ).astype(BF16)
    highest_ref[...] = highest
    totals_ref[...] = totals
    lines = turned_ref.shape[0] // angles_here
    for angle in range(angles_here):
        average_ref[angle * total : (angle + 1) * total, :] = averages[
            :, angle * lines : (angle + 1) * lines
        ]
    kept = theirs_ref.shape[0]
    terms = jnp.dot(harmonic_ref[kept:, :], average_ref[...], preferred_element_type=F32)
    theirs_ref[...] = terms.astype(theirs_ref.dtype)


def own_body(average_ref, harmonic_ref, mine_ref):
    kept = mine_ref.shape[0]
    mine_ref[...] = jnp.dot(harmonic_ref[:kept, :], average_ref[...], preferred_element_type=F32)


def pair_body(mine_ref, other_ref, *out_refs):
    span = out_refs[0].shape[0]
    for turn, out_ref in enumerate(out_refs):
        rows = slice(turn * span, (turn + 1) * span)
        out_ref[...] = (mine_ref[rows, :] + other_ref[rows, :].astype(F32)).astype(out_ref.dtype)


def last_body(highest_ref, totals_ref, *refs):
    evidence_ref, out_ref = refs[-2:]
    evidence_ref[...] = highest_ref[...] + jnp.log(totals_ref[...])
    total = refs[0][...]
    for ref in refs[1:-2]:
        total = total + ref[...].astype(F32)
    out_ref[...] = total.T


def params(limit, **more):
    return pltpu.CompilerParams(vmem_limit_bytes=int(min(limit, 60 * MIB)), **more)


def in_hbm(array):
    return pltpu.with_memory_space_constraint(array, pltpu.HBM)


def swap(array, axis, size, turn):
    return lax.ppermute(array, axis, [(i, i ^ turn) for i in range(size)])


def spread(arrays):
    out = [arrays[0]]
    for turn in range(1, len(arrays)):
        out.append(swap(arrays[turn], "rot", len(arrays), turn))
    return out


def steps(
    images, references, noise_weight, euler_angles, candidate_count, candidate_rotation, image_order
):
    owners = lax.axis_size("rot")
    angle_parts = lax.axis_size("ang")
    shell_parts = lax.axis_size("shell")
    parts, shells_here, angles_here, images_here = images.shape
    lines = parts * shells_here
    features = lines * angles_here
    rotations_here = references.shape[3]
    blocks_here, _, slots = candidate_rotation.shape
    total = owners * slots
    wide = features + LANES
    columns = angles_here * total
    span = COEF // (owners * angle_parts)
    link = BF16

    if owners <= SUBLANES:
        request = jnp.concatenate(
            [
                candidate_rotation,
                jnp.pad(candidate_count[:, None, :], ((0, 0), (0, 0), (0, slots - owners))),
            ],
            axis=1,
        )
        requests = spread([request] * owners)
    else:
        request = jnp.concatenate([candidate_rotation, candidate_count[:, :, None]], axis=2)
        requests = [lax.all_to_all(jnp.swapaxes(request, 0, 1), "rot", 0, 0, tiled=True)]
    table, mask = pl.pallas_call(
        functools.partial(stage_body, images_here // blocks_here),
        out_shape=[struct((wide, rotations_here), BF16), struct((total, images_here), F32)],
        in_specs=[HBM] * 4,
        out_specs=[VMEM] * 2,
        scratch_shapes=[
            pltpu.VMEM((3, rotations_here), F32),
            pltpu.VMEM((1, images_here), I32),
            pltpu.VMEM((blocks_here, owners), I32),
            pltpu.SemaphoreType.DMA((3 + STAGES,)),
        ],
        cost_estimate=pl.CostEstimate(
            flops=wide * rotations_here, bytes_accessed=4 * wide * rotations_here, transcendentals=0
        ),
        compiler_params=params(wide * rotations_here * 2 + total * images_here * 8 + 4 * MIB),
        name="stage",
    )(
        in_hbm(references.reshape(features, rotations_here)),
        in_hbm(euler_angles),
        in_hbm(image_order[None]),
        in_hbm(candidate_count),
    )
    chosen = pl.pallas_call(
        functools.partial(select_body, len(requests)),
        out_shape=[struct((slots, wide), BF16)] * owners,
        in_specs=[VMEM] * (len(requests) + 1),
        out_specs=[VMEM] * owners,
        compiler_params=params(wide * rotations_here * 2 + total * wide * 8 + 4 * MIB),
        name="select",
    )(*requests, table)
    slices = spread(chosen)

    chunk = 16
    natural, turned = pl.pallas_call(
        functools.partial(weigh_body, angles_here, chunk),
        out_shape=[
            struct((features, images_here), BF16),
            struct((angles_here, lines, images_here), BF16),
        ],
        in_specs=[SMEM, HBM],
        out_specs=[VMEM] * 2,
        scratch_shapes=[
            pltpu.VMEM((features, images_here), F32),
            pltpu.SemaphoreType.DMA((lines // chunk,)),
        ],
        cost_estimate=pl.CostEstimate(
            flops=4 * features * images_here, bytes_accessed=8 * features * images_here, transcendentals=0
        ),
        compiler_params=params(features * images_here * 8 + 4 * MIB),
        name="weigh",
    )(noise_weight, in_hbm(images.reshape(features, images_here)))

    noise_row = jnp.broadcast_to(
        noise_weight[None, :, None], (parts, shells_here, angles_here)
    ).reshape(1, features)
    partial = pl.pallas_call(
        score_body,
        out_shape=struct((total, images_here), F32),
        in_specs=[VMEM] * (2 + owners),
        out_specs=VMEM,
        compiler_params=params(features * images_here * 2 + total * wide * 12 + 4 * MIB),
        name="score",
    )(noise_row, natural, *slices)

    count = shell_parts * angle_parts
    shares = [partial]
    if STAGED:
        turn = 1
        while turn < count:
            shares.append(
                lax.ppermute(shares[0], ("shell", "ang"), [(i, i ^ turn) for i in range(count)])
            )
            turn *= 2
            if turn < count:
                shares = [
                    pl.pallas_call(
                        add_body,
                        out_shape=struct((total, images_here), F32),
                        in_specs=[VMEM] * 2,
                        out_specs=VMEM,
                        compiler_params=params(total * images_here * 12 + 2 * MIB),
                        name="add",
                    )(*shares)
                ]
    else:
        for turn in range(1, count):
            shares.append(
                lax.ppermute(partial, ("shell", "ang"), [(i, i ^ turn) for i in range(count)])
            )

    harmonics = pl.pallas_call(
        functools.partial(harmonic_body, total, angles_here, owners, angle_parts),
        grid=(columns // TILE,),
        out_shape=struct((COEF, columns), BF16),
        in_specs=[VMEM] * owners,
        out_specs=pl.BlockSpec((COEF, TILE), lambda i: (0, i)),
        scratch_shapes=[pltpu.VMEM((COEF * SUBLANES, LANES), F32)],
        cost_estimate=pl.CostEstimate(
            flops=8 * COEF * columns, bytes_accessed=2 * COEF * columns, transcendentals=6 * columns
        ),
        compiler_params=params(12 * MIB),
        name="harmonics",
    )(*slices)

    kept = COEF // angle_parts
    highest, totals, averages, theirs = pl.pallas_call(
        functools.partial(average_body, angles_here),
        out_shape=[
            struct((1, images_here), F32),
            struct((1, images_here), F32),
            struct((columns, lines), BF16),
            struct((kept, lines), link),
        ],
        in_specs=[VMEM] * (3 + len(shares)),
        out_specs=[VMEM] * 4,
        compiler_params=params(
            features * images_here * 2 + COEF * columns * 2 + total * features * 8
            + columns * lines * 4 + COEF * lines * 12 + 4 * MIB
        ),
        name="average",
    )(mask, turned.reshape(features, images_here), harmonics, *shares)
    other = swap(theirs, "ang", angle_parts, 1)
    mine = pl.pallas_call(
        own_body,
        out_shape=struct((kept, lines), F32),
        in_specs=[VMEM] * 2,
        out_specs=VMEM,
        cost_estimate=pl.CostEstimate(
            flops=2 * kept * columns * lines, bytes_accessed=4 * kept * columns, transcendentals=0
        ),
        compiler_params=params(COEF * columns * 2 + columns * lines * 4 + COEF * lines * 8 + 4 * MIB),
        name="own",
    )(averages, harmonics)
    sums = pl.pallas_call(
        pair_body,
        out_shape=[struct((span, lines), F32)] + [struct((span, lines), link)] * (owners - 1),
        in_specs=[VMEM] * 2,
        out_specs=[VMEM] * owners,
        compiler_params=params(COEF * lines * 8 + 4 * MIB),
        name="pair",
    )(mine, other)
    pieces = spread(sums)
    evidence, coefficients = pl.pallas_call(
        last_body,
        out_shape=[struct((1, images_here), F32), struct((lines, span), F32)],
        in_specs=[VMEM] * (2 + owners),
        out_specs=[VMEM] * 2,
        compiler_params=params(COEF * lines * 4 + 4 * MIB),
        name="last",
    )(highest, totals, *pieces)
    coefficients = jnp.transpose(coefficients.reshape(parts, shells_here, span), (2, 0, 1))
    return coefficients, evidence.reshape(images_here)


def solution(mesh):
    in_specs = (
        P(None, "shell", "ang", ("grp", "rot")),
        P(None, "shell", "ang", ("grp", "rot")),
        P(("grp", "shell")),
        P(None, ("grp", "rot")),
        P(("grp", "rot"), None),
        P(("grp", "rot"), None, None),
        P(("grp", "rot")),
    )
    out_specs = (P(("grp", "rot", "ang"), None, "shell"), P(("grp", "rot")))
    return jax.shard_map(steps, mesh=mesh, in_specs=in_specs, out_specs=out_specs, check_vma=False)
```

```python
import functools
import math

import jax
import jax.numpy as jnp
from jax import lax
from jax.experimental import pallas as pl
from jax.experimental.pallas import tpu as pltpu
from jax.sharding import PartitionSpec as P


ORDER = 32
COEF = ORDER * ORDER
LANES = 128
SUBLANES = 8
TILE = SUBLANES * LANES
MIB = 1 << 20
STAGES = 16


SMEM = pl.BlockSpec(memory_space=pltpu.SMEM)
VMEM = pl.BlockSpec(memory_space=pltpu.VMEM)
HBM = pl.BlockSpec(memory_space=pltpu.HBM)
F32 = jnp.float32
BF16 = jnp.bfloat16
I32 = jnp.int32


def struct(shape, dtype):
    return jax.ShapeDtypeStruct(shape, dtype)


def iota(shape, dim):
    return lax.broadcasted_iota(I32, shape, dim)


def stage_body(
    block_size, reference_ref, angle_ref, order_ref, count_ref, table_ref, mask_ref,
    euler_here, order_here, count_here, sems
):
    features, rotations = reference_ref.shape
    small = [
        pltpu.make_async_copy(angle_ref, euler_here, sems.at[0]),
        pltpu.make_async_copy(order_ref, order_here, sems.at[1]),
        pltpu.make_async_copy(count_ref, count_here, sems.at[2]),
    ]
    for copy in small:
        copy.start()
    size = features // STAGES
    large = [
        pltpu.make_async_copy(
            reference_ref.at[pl.ds(part * size, size), :],
            table_ref.at[pl.ds(part * size, size), :],
            sems.at[3 + part],
        )
        for part in range(STAGES)
    ]
    for copy in large:
        copy.start()
    for copy in small:
        copy.wait()
    line = iota((SUBLANES, rotations), 0)
    rest = jnp.where(
        line == 0,
        euler_here[0:1, :],
        jnp.where(line == 1, euler_here[1:2, :], jnp.where(line == 2, euler_here[2:3, :], 0.0)),
    )
    terms = []
    for _ in range(3):
        term = rest.astype(BF16).astype(F32)
        terms.append(term)
        rest = rest - term
    terms.append(jnp.zeros((LANES - 3 * SUBLANES, rotations), F32))
    table_ref[features:, :] = jnp.concatenate(terms, axis=0).astype(BF16)

    images = order_here.shape[1]
    same = jnp.where(order_here[...] == iota((images, images), 0), 1.0, 0.0).astype(BF16)
    block_of = (iota((SUBLANES, images), 1) // block_size).astype(F32).astype(BF16)
    image_block = lax.dot_general(
        block_of, same, (((1,), (1,)), ((), ())), preferred_element_type=F32
    )[0:1, :]
    blocks, owners = count_here.shape
    slots = mask_ref.shape[0] // owners
    me = lax.axis_index("rot")
    position = iota((slots, images), 0).astype(F32)
    counts = count_here[...].astype(F32)
    lane = iota((blocks, owners), 1)
    for turn in range(owners):
        listed = jnp.sum(
            jnp.where(lane == lax.bitwise_xor(me, turn), counts, 0.0), axis=1, keepdims=True
        )
        mask = jnp.full((slots, images), -jnp.inf, F32)
        start = jnp.zeros((1, 1), F32)
        for block in range(blocks):
            stop = start + listed[block : block + 1, :]
            inside = (position >= start) & (position < stop) & (image_block == block)
            mask = jnp.where(inside, 0.0, mask)
            start = stop
        mask_ref[turn * slots : (turn + 1) * slots, :] = mask
    for copy in large:
        copy.wait()


def select_body(asked, *refs):
    request_refs = refs[:asked]
    table_ref = refs[asked]
    out_refs = refs[asked + 1 :]
    owners = len(out_refs)
    rotations = table_ref.shape[1]
    slots = out_refs[0].shape[0]
    me = lax.axis_index("rot")
    direct = asked == owners
    blocks = request_refs[0].shape[0 if direct else 1]
    rows = []
    counts = []
    for turn in range(owners):
        for block in range(blocks):
            if direct:
                rows.append(request_refs[turn][block, pl.ds(me, 1), :])
                counts.append(request_refs[turn][block, owners : owners + 1, :])
            else:
                both = request_refs[0][lax.bitwise_xor(me, turn), block : block + 1, :]
                rows.append(both[:, :slots])
                counts.append(both[:, slots:])
    counts = jnp.concatenate(counts, axis=0).astype(F32)
    if direct:
        counts = jnp.sum(jnp.where(iota(counts.shape, 1) == me, counts, 0.0), axis=1, keepdims=True)
    to = iota((slots, slots), 0).astype(F32)
    entry = iota((slots, slots), 1).astype(F32)
    groups = []
    for turn in range(owners):
        group = jnp.zeros((slots, slots), F32)
        start = jnp.zeros((1, 1), F32)
        for block in range(blocks):
            place = turn * blocks + block
            count = counts[place : place + 1, :]
            inside = (to == entry + start) & (entry < count)
            group = group + jnp.where(inside, rows[place].astype(F32) + 1.0, 0.0)
            start = start + count
        groups.append(group)
    wanted = jnp.sum(jnp.concatenate(groups, axis=0), axis=1, keepdims=True)
    lane = iota((owners * slots, rotations), 1).astype(F32) + 1.0
    chosen = jnp.where(wanted == lane, 1.0, 0.0).astype(BF16)
    picked = lax.dot_general(
        chosen, table_ref[...], (((1,), (1,)), ((), ())), preferred_element_type=F32
    )
    for turn, out_ref in enumerate(out_refs):
        out_ref[...] = picked[turn * slots : (turn + 1) * slots].astype(BF16)


def weigh_body(angles_here, chunk, noise_ref, image_ref, natural_ref, turned_ref, held_ref, sems):
    features, images = image_ref.shape
    shells = noise_ref.shape[0]
    size = chunk * angles_here
    steps = features // size

    def copy(step):
        rows = pl.ds(pl.multiple_of(step * size, size), size)
        return pltpu.make_async_copy(image_ref.at[rows, :], held_ref.at[rows, :], sems.at[step])

    for step in range(steps):
        copy(step).start()

    def one_chunk(step, carry):
        copy(step).wait()
        for side in range(images // LANES):
            lanes = slice(side * LANES, (side + 1) * LANES)
            planes = []
            for line in range(chunk):
                weight = noise_ref[lax.rem(step * chunk + line, shells)]
                rows = pl.ds(
                    pl.multiple_of((step * chunk + line) * angles_here, angles_here), angles_here
                )
                plane = held_ref[rows, lanes] * weight
                natural_ref[rows, lanes] = plane.astype(BF16)
                planes.append(plane)
            turned_ref[:, pl.ds(pl.multiple_of(step * chunk, chunk), chunk), lanes] = jnp.swapaxes(
                jnp.stack(planes, axis=0), 0, 1
            ).astype(BF16)
        return carry

    lax.fori_loop(0, steps, one_chunk, 0)


def score_body(noise_ref, natural_ref, *refs):
    slice_refs = refs[:-2]
    score_ref, euler_ref = refs[-2:]
    features = natural_ref.shape[0]
    slices = jnp.concatenate([ref[:, :features].astype(F32) for ref in slice_refs], axis=0)
    norms = jnp.sum(slices * slices * noise_ref[...], axis=1, keepdims=True)
    products = jnp.dot(slices.astype(BF16), natural_ref[...], preferred_element_type=F32)
    score_ref[...] = 2.0 * products - norms
    terms = jnp.concatenate([ref[:, features:].astype(F32) for ref in slice_refs], axis=0)
    slots = terms.shape[0]
    terms = terms.astype(BF16)
    repeats = max(1, slots // LANES)
    line = iota((SUBLANES, LANES), 0)
    planes = [jnp.zeros((SUBLANES, LANES), F32)] * 3
    for repeat in range(repeats):
        place = lax.rem(repeat * LANES + iota((slots, LANES), 1), slots)
        spread = jnp.where(place == iota((slots, LANES), 0), 1.0, 0.0).astype(BF16)
        rows = lax.dot_general(
            terms, spread, (((0,), (0,)), ((), ())), preferred_element_type=F32
        )
        whole = rows[:8] + rows[8:16] + rows[16:24]
        here = lax.rem(line, repeats) == repeat
        planes = [
            jnp.where(here, whole[axis : axis + 1, :], planes[axis]) for axis in range(3)
        ]
    for axis in range(3):
        euler_ref[axis] = planes[axis]


def harmonic_constants():
    first = {}
    second = {}
    for degree in range(ORDER):
        for azimuth in range(degree):
            first[degree, azimuth] = math.sqrt(
                (4.0 * degree * degree - 1.0) / (degree * degree - azimuth * azimuth)
            )
            lower = max((degree - 1.0) ** 2 - azimuth * azimuth, 0.0)
            second[degree, azimuth] = math.sqrt(lower / max(4.0 * (degree - 1.0) ** 2 - 1.0, 1.0))
    diagonal = []
    running = 1.0
    for degree in range(ORDER):
        if degree > 0:
            running = running * (2.0 * degree - 1.0) / (2.0 * degree)
        diagonal.append(math.sqrt((2.0 * degree + 1.0) / (4.0 * math.pi) * running))
    return first, second, diagonal


def harmonic_body(slots, angles_here, owners, angle_parts, euler_ref, out_ref, rows_ref):
    first, second, diagonal = harmonic_constants()
    tile = (SUBLANES, LANES)
    column = pl.program_id(0) * TILE + iota(tile, 0) * LANES + iota(tile, 1)
    angle = lax.axis_index("ang") * angles_here + column // slots
    phase = 2.0 * math.pi / (angles_here * angle_parts) * angle.astype(F32) + euler_ref[2]
    cos_phase = jnp.cos(phase)
    sin_phase = jnp.sin(phase)
    cos_alpha = jnp.cos(euler_ref[0])
    sin_alpha = jnp.sin(euler_ref[0])
    cos_beta = jnp.cos(euler_ref[1])
    sin_beta = jnp.sin(euler_ref[1])
    along_x = cos_alpha * cos_beta * cos_phase - sin_alpha * sin_phase
    along_y = sin_alpha * cos_beta * cos_phase + cos_alpha * sin_phase
    along_z = -sin_beta * cos_phase

    def put(index, value):
        rows_ref[index * SUBLANES : (index + 1) * SUBLANES, :] = value

    real_part = jnp.ones(tile, F32)
    imag_part = jnp.zeros(tile, F32)
    for azimuth in range(ORDER):
        real_scaled = real_part * math.sqrt(2.0)
        imag_scaled = imag_part * math.sqrt(2.0)
        earlier = None
        current = None
        for degree in range(azimuth, ORDER):
            if degree == azimuth:
                value = jnp.full(tile, diagonal[azimuth], F32)
            elif degree == azimuth + 1:
                value = (first[degree, azimuth] * along_z) * current
            else:
                value = first[degree, azimuth] * (
                    along_z * current - second[degree, azimuth] * earlier
                )
            earlier, current = current, value
            if azimuth == 0:
                put(degree * degree, value)
            else:
                put(degree * degree + 2 * azimuth - 1, value * real_scaled)
                put(degree * degree + 2 * azimuth, value * imag_scaled)
        real_part, imag_part = (
            along_x * real_part - along_y * imag_part,
            along_x * imag_part + along_y * real_part,
        )
    me = lax.axis_index("rot")
    here = lax.axis_index("ang")
    span = COEF // (owners * angle_parts)
    for owner in range(owners):
        for ang in range(angle_parts):
            side = lax.rem(here + ang, angle_parts)
            place = (side * owners + lax.bitwise_xor(me, owner)) * span
            rows = pl.ds(pl.multiple_of(place, span), span)
            start = (owner * angle_parts + ang) * span * SUBLANES
            for part in range(SUBLANES):
                out_ref[rows, part * LANES : (part + 1) * LANES] = rows_ref[
                    pl.ds(start + part, span, stride=SUBLANES), :
                ].astype(BF16)


def average_body(angles_here, mask_ref, turned_ref, harmonic_ref, *refs):
    highest_ref, totals_ref, average_ref, theirs_ref = refs[-4:]
    sums = [ref[...] for ref in refs[:-4]]
    while len(sums) > 1:
        sums = [sums[i] + sums[i + 1] for i in range(0, len(sums), 2)]
    masked = sums[0] + mask_ref[...]
    total = masked.shape[0]
    highest = jnp.max(masked, axis=0, keepdims=True)
    shares = jnp.exp(masked - highest)
    totals = jnp.sum(shares, axis=0, keepdims=True)
    weights = (shares / totals).astype(BF16)
    averages = lax.dot_general(
        weights, turned_ref[...], (((1,), (1,)), ((), ())), preferred_element_type=F32
    ).astype(BF16)
    highest_ref[...] = highest
    totals_ref[...] = totals
    lines = turned_ref.shape[0] // angles_here
    for angle in range(angles_here):
        average_ref[angle * total : (angle + 1) * total, :] = averages[
            :, angle * lines : (angle + 1) * lines
        ]
    kept = theirs_ref.shape[0]
    terms = jnp.dot(harmonic_ref[kept:, :], average_ref[...], preferred_element_type=F32)
    theirs_ref[...] = terms.astype(theirs_ref.dtype)


def own_body(highest_ref, totals_ref, average_ref, harmonic_ref, evidence_ref, mine_ref):
    evidence_ref[...] = highest_ref[...] + jnp.log(totals_ref[...])
    kept = mine_ref.shape[0]
    mine_ref[...] = jnp.dot(harmonic_ref[:kept, :], average_ref[...], preferred_element_type=F32)


def pair_body(mine_ref, other_ref, *out_refs):
    span = out_refs[0].shape[0]
    for turn, out_ref in enumerate(out_refs):
        rows = slice(turn * span, (turn + 1) * span)
        out_ref[...] = (mine_ref[rows, :] + other_ref[rows, :].astype(F32)).astype(out_ref.dtype)


def last_body(*refs):
    out_ref = refs[-1]
    total = refs[0][...]
    for ref in refs[1:-1]:
        total = total + ref[...].astype(F32)
    out_ref[...] = total.T


def params(limit, **more):
    return pltpu.CompilerParams(vmem_limit_bytes=int(min(limit, 60 * MIB)), **more)


def in_hbm(array):
    return pltpu.with_memory_space_constraint(array, pltpu.HBM)


def swap(array, axis, size, turn):
    return lax.ppermute(array, axis, [(i, i ^ turn) for i in range(size)])


def spread(arrays):
    out = [arrays[0]]
    for turn in range(1, len(arrays)):
        out.append(swap(arrays[turn], "rot", len(arrays), turn))
    return out


def steps(
    images, references, noise_weight, euler_angles, candidate_count, candidate_rotation, image_order
):
    owners = lax.axis_size("rot")
    angle_parts = lax.axis_size("ang")
    shell_parts = lax.axis_size("shell")
    parts, shells_here, angles_here, images_here = images.shape
    lines = parts * shells_here
    features = lines * angles_here
    rotations_here = references.shape[3]
    blocks_here, _, slots = candidate_rotation.shape
    total = owners * slots
    wide = features + LANES
    columns = angles_here * total
    span = COEF // (owners * angle_parts)
    link = BF16

    if owners <= SUBLANES:
        request = jnp.concatenate(
            [
                candidate_rotation,
                jnp.pad(candidate_count[:, None, :], ((0, 0), (0, 0), (0, slots - owners))),
            ],
            axis=1,
        )
        requests = [request] + [swap(request, "rot", owners, k) for k in range(1, owners)]
    else:
        request = jnp.concatenate([candidate_rotation, candidate_count[:, :, None]], axis=2)
        requests = [lax.all_to_all(jnp.swapaxes(request, 0, 1), "rot", 0, 0, tiled=True)]
    table, mask = pl.pallas_call(
        functools.partial(stage_body, images_here // blocks_here),
        out_shape=[struct((wide, rotations_here), BF16), struct((total, images_here), F32)],
        in_specs=[HBM] * 4,
        out_specs=[VMEM] * 2,
        scratch_shapes=[
            pltpu.VMEM((3, rotations_here), F32),
            pltpu.VMEM((1, images_here), I32),
            pltpu.VMEM((blocks_here, owners), I32),
            pltpu.SemaphoreType.DMA((3 + STAGES,)),
        ],
        cost_estimate=pl.CostEstimate(
            flops=wide * rotations_here, bytes_accessed=4 * wide * rotations_here, transcendentals=0
        ),
        compiler_params=params(wide * rotations_here * 2 + total * images_here * 8 + 4 * MIB),
        name="stage",
    )(
        in_hbm(references.reshape(features, rotations_here)),
        in_hbm(euler_angles),
        in_hbm(image_order[None]),
        in_hbm(candidate_count),
    )
    chosen = pl.pallas_call(
        functools.partial(select_body, len(requests)),
        out_shape=[struct((slots, wide), BF16)] * owners,
        in_specs=[VMEM] * (len(requests) + 1),
        out_specs=[VMEM] * owners,
        compiler_params=params(wide * rotations_here * 2 + total * wide * 8 + 4 * MIB),
        name="select",
    )(*requests, table)
    slices = spread(chosen)

    chunk = 16
    natural, turned = pl.pallas_call(
        functools.partial(weigh_body, angles_here, chunk),
        out_shape=[
            struct((features, images_here), BF16),
            struct((angles_here, lines, images_here), BF16),
        ],
        in_specs=[SMEM, HBM],
        out_specs=[VMEM] * 2,
        scratch_shapes=[
            pltpu.VMEM((features, images_here), F32),
            pltpu.SemaphoreType.DMA((lines // chunk,)),
        ],
        cost_estimate=pl.CostEstimate(
            flops=4 * features * images_here, bytes_accessed=8 * features * images_here, transcendentals=0
        ),
        compiler_params=params(features * images_here * 8 + 4 * MIB),
        name="weigh",
    )(noise_weight, in_hbm(images.reshape(features, images_here)))

    noise_row = jnp.broadcast_to(
        noise_weight[None, :, None], (parts, shells_here, angles_here)
    ).reshape(1, features)
    partial, eulers = pl.pallas_call(
        score_body,
        out_shape=[struct((total, images_here), F32), struct((3, SUBLANES, LANES), F32)],
        in_specs=[VMEM] * (2 + owners),
        out_specs=[VMEM] * 2,
        compiler_params=params(features * images_here * 2 + total * wide * 12 + 4 * MIB),
        name="score",
    )(noise_row, natural, *slices)

    count = shell_parts * angle_parts
    shares = [partial] + [
        lax.ppermute(partial, ("shell", "ang"), [(i, i ^ k) for i in range(count)])
        for k in range(1, count)
    ]

    harmonics = pl.pallas_call(
        functools.partial(harmonic_body, total, angles_here, owners, angle_parts),
        grid=(columns // TILE,),
        out_shape=struct((COEF, columns), BF16),
        in_specs=[pl.BlockSpec((3, SUBLANES, LANES), lambda i: (0, 0, 0))],
        out_specs=pl.BlockSpec((COEF, TILE), lambda i: (0, i)),
        scratch_shapes=[pltpu.VMEM((COEF * SUBLANES, LANES), F32)],
        cost_estimate=pl.CostEstimate(
            flops=8 * COEF * columns, bytes_accessed=2 * COEF * columns, transcendentals=6 * columns
        ),
        compiler_params=params(12 * MIB),
        name="harmonics",
    )(eulers)

    kept = COEF // angle_parts
    highest, totals, averages, theirs = pl.pallas_call(
        functools.partial(average_body, angles_here),
        out_shape=[
            struct((1, images_here), F32),
            struct((1, images_here), F32),
            struct((columns, lines), BF16),
            struct((kept, lines), link),
        ],
        in_specs=[VMEM] * (3 + count),
        out_specs=[VMEM] * 4,
        compiler_params=params(
            features * images_here * 2 + COEF * columns * 2 + total * features * 8
            + columns * lines * 4 + COEF * lines * 12 + 4 * MIB
        ),
        name="average",
    )(mask, turned.reshape(features, images_here), harmonics, *shares)
    other = swap(theirs, "ang", angle_parts, 1)
    evidence, mine = pl.pallas_call(
        own_body,
        out_shape=[struct((1, images_here), F32), struct((kept, lines), F32)],
        in_specs=[VMEM] * 4,
        out_specs=[VMEM] * 2,
        cost_estimate=pl.CostEstimate(
            flops=2 * kept * columns * lines, bytes_accessed=4 * kept * columns, transcendentals=0
        ),
        compiler_params=params(COEF * columns * 2 + columns * lines * 4 + COEF * lines * 8 + 4 * MIB),
        name="own",
    )(highest, totals, averages, harmonics)
    sums = pl.pallas_call(
        pair_body,
        out_shape=[struct((span, lines), F32)] + [struct((span, lines), link)] * (owners - 1),
        in_specs=[VMEM] * 2,
        out_specs=[VMEM] * owners,
        compiler_params=params(COEF * lines * 8 + 4 * MIB),
        name="pair",
    )(mine, other)
    pieces = spread(sums)
    coefficients = pl.pallas_call(
        last_body,
        out_shape=struct((lines, span), F32),
        in_specs=[VMEM] * owners,
        out_specs=VMEM,
        compiler_params=params(COEF * lines * 4 + 4 * MIB),
        name="last",
    )(*pieces)
    coefficients = jnp.transpose(coefficients.reshape(parts, shells_here, span), (2, 0, 1))
    return coefficients, evidence.reshape(images_here)


def solution(mesh):
    in_specs = (
        P(None, "shell", "ang", ("grp", "rot")),
        P(None, "shell", "ang", ("grp", "rot")),
        P(("grp", "shell")),
        P(None, ("grp", "rot")),
        P(("grp", "rot"), None),
        P(("grp", "rot"), None, None),
        P(("grp", "rot")),
    )
    out_specs = (P(("grp", "rot", "ang"), None, "shell"), P(("grp", "rot")))
    return jax.shard_map(steps, mesh=mesh, in_specs=in_specs, out_specs=out_specs, check_vma=False)
```
